128 devices in a mesh: space: 8 (over y, x_lo), mode: 16 (over x_hi, z, core).
Axes of the slice: x: 4 (x_hi: 2, x_lo: 2; x = x_hi * 2 + x_lo), y: 4, z: 4, core: 2. Of those that a mesh axis runs over, the one named last changes fastest.
Arguments:
- source_field: float32 [16, 4, 128, 4096], P('space', None, None, 'mode'), may hold values from -6 to 6
- mean_operator: float32 [16, 4, 128, 896], P('space'), may hold values from -0.109375 to 0.109375
- field_operators: float32 [4, 16, 4, 128, 896], P(None, 'space'), may hold values from -0.078125 to 0.078125
- adjacency: int32 [16, 4, 4], P('space'), may hold values from 0 to 3
- mode_masks: int32 [4], replicated, may hold values from 256 to 2048, as said below
Outputs:
- solution_field: float32 [16, 4, 128, 4096], P('space', None, None, 'mode')
- residual: float32 [16, 4, 128, 4096], P('space', None, None, 'mode')
The draws below stay inside these ranges and needn't reach their ends.
Inputs may be any that keep to these rules, and one draw needn't show every extreme that they name: `mode_masks`: each value is 256 times a power of two, at most 2048, and every such value belongs to at least one field.
All inputs are finite; a program needn't handle non-finite values.
Results may differ from the reference program's by a relative error of at most 0.0001.
Values sent between devices are 32-bit elements; how exact they have to be, the bound alone decides.
No kernel may reach another device: no remote copies, remote signals or barrier semaphores. Data moves between devices by JAX's collectives and lax.ppermute only.
A program may use at most 128 MiB of HBM per device.

```python
import jax
import jax.numpy as jnp
from jax import lax

BLK = 128
MODE_DEV = 256
MODES = 4096
NF = 4
FACE = 4
LAYERS = 16
DEGREE = 4


def draw_mode_masks(key, part):
    bit_count = (MODES // MODE_DEV).bit_length() - 1
    order = jax.random.permutation(jax.random.fold_in(key, 11), NF)
    extra = jax.random.randint(jax.random.fold_in(key, 12), (NF,), 0, bit_count)
    slots = jnp.arange(NF, dtype=jnp.int32)
    slot_bits = jnp.where(slots < bit_count, slots, extra)
    field_bits = slot_bits[order]
    return (MODE_DEV * jnp.left_shift(jnp.ones((NF,), jnp.int32), field_bits)).astype(jnp.int32)


def with_ends(values, rng, low, largest):
    shape = values.shape
    index_at = [jax.random.randint(jax.random.fold_in(rng, axis), (), 0, shape[axis]) for axis in range(len(shape))]
    values = values.at[tuple(index_at)].set(low)
    longest = shape.index(max(shape))
    index_at[longest] = (index_at[longest] + 1) % shape[longest]
    return values.at[tuple(index_at)].set(largest)


def level_of(key, shape, pieces, low, top_value):
    loudness, own = 1.0, jax.random.fold_in(key, 6)
    for axis_at, shards_of in pieces:
        draws = jnp.exp(jax.random.uniform(jax.random.fold_in(own, axis_at), (shards_of,), jnp.float32, low / len(pieces), top_value / len(pieces)))
        loudness = loudness * jnp.repeat(draws, shape[axis_at] // shards_of).reshape([-1 if axis == axis_at else 1 for axis in range(len(shape))])
    return loudness


def gaussian(own_key, shape, deviation, limit, split=(), kind=jnp.bfloat16):
    factor_of = level_of(own_key, shape, split, -0.22, 0.18) if split else 1.0
    array = jax.random.normal(own_key, shape, jnp.float32) * deviation * factor_of
    return jnp.minimum(jnp.maximum(array, -limit), limit).astype(kind)


def setup_inputs(seed: int = 0) -> dict:
    streams_of = jax.random.split(jax.random.key(seed), 6)
    return {
        "source_field": gaussian(streams_of[0], (LAYERS, FACE, BLK, MODES), 1.0, 6.0, ((0, 8), (3, 16)), jnp.float32),
        "mean_operator": gaussian(streams_of[1], (LAYERS, FACE, BLK, 7 * BLK), 0.007, 0.109375, ((0, 8),), jnp.float32),
        "field_operators": gaussian(streams_of[2], (NF, LAYERS, FACE, BLK, 7 * BLK), 0.005, 0.078125, ((1, 8),), jnp.float32),
        "adjacency": with_ends(jax.random.randint(streams_of[3], (LAYERS, FACE, 4), 0, FACE), jax.random.fold_in(streams_of[3], 1), 0, FACE - 1).astype(jnp.int32),
        "mode_masks": draw_mode_masks(jax.random.fold_in(streams_of[5], 71), 0),
    }


coupling_coef = 0.5773502691896258
theta_value = 1.0
delta_value = 0.7


def operate_on(field, mean_operator, field_operators, adjacency, mode_masks):
    padded = jnp.pad(field, ((1, 1), (0, 0), (0, 0), (0, 0)))
    mode_index = jnp.arange(field.shape[3], dtype=jnp.int32)

    def one_layer(layer_index):
        window = lax.dynamic_slice_in_dim(padded, layer_index, 3, 0)
        centre = window[1]
        neighbours = adjacency[layer_index]
        in_layer = centre[neighbours]
        stacked = jnp.concatenate([centre[:, None], window[0][:, None], window[2][:, None], in_layer], axis=1)
        columns = stacked.reshape(FACE, 7 * BLK, field.shape[3])
        result = centre + jnp.einsum("fij,fjm->fim", mean_operator[layer_index], columns, precision=lax.Precision.HIGHEST)
        for field_number in range(NF):
            term = jnp.einsum("fij,fjm->fim", field_operators[field_number, layer_index], columns, precision=lax.Precision.HIGHEST)
            partner = jnp.bitwise_xor(mode_index, mode_masks[field_number])
            result = result + coupling_coef * jnp.take(term, partner, axis=2)
        return result

    return lax.map(one_layer, jnp.arange(LAYERS, dtype=jnp.int32))


def reference(source_field, mean_operator, field_operators, adjacency, mode_masks):
    sigma_value = theta_value / delta_value
    solution_field = jnp.zeros_like(source_field)
    residual = source_field
    direction = source_field / theta_value
    ratio_now = jnp.asarray(1.0 / sigma_value, dtype=jnp.float32)

    def iterate_once(count, carry):
        solution_field, residual, direction, ratio_now = carry
        solution_field = solution_field + direction
        residual = residual - operate_on(direction, mean_operator, field_operators, adjacency, mode_masks)
        ratio_new = 1.0 / (2.0 * sigma_value - ratio_now)
        direction = ratio_new * ratio_now * direction + (2.0 * ratio_new / delta_value) * residual
        return solution_field, residual, direction, ratio_new

    solution_field, residual, direction, ratio_now = lax.fori_loop(0, DEGREE, iterate_once, (solution_field, residual, direction, ratio_now))
    return solution_field, residual
```

```python
import functools

import jax
import jax.numpy as jnp
from jax import lax
from jax.experimental import pallas as pl
from jax.experimental.pallas import tpu as pltpu
from jax.sharding import PartitionSpec as P

DEGREE = 4
COUPLING = 0.5773502691896258
THETA = 1.0
DELTA = 0.7
AXES = ("space", "mode")
F32 = jnp.float32
BF16 = jnp.bfloat16
NT = (((1,), (1,)), ((), ()))


def split2(value):
    high = value.astype(BF16)
    return high, (value - high.astype(F32)).astype(BF16)


def dot_nt(left, right):
    return lax.dot_general(left, right, NT, preferred_element_type=F32)


def swap_rows(value, bit, group):
    step = group << bit
    count = value.shape[0] // step
    return jnp.concatenate(
        [value[(i ^ 1) * step : (i ^ 1) * step + step] for i in range(count)], axis=0
    )


def permuted(value, op, group):
    return value if op == 0 else swap_rows(value, op - 1, group)


def split_kernel(where_ref, field_ref, out_ref):
    pieces, layers, faces, group, blk = out_ref.shape
    half = pieces // 2
    first = where_ref[0] * half
    second = half - first
    lead = where_ref[1]
    for l in range(layers):
        at = lead if l == 0 else 1 - lead
        for f in range(faces):
            rows = field_ref[at, f].T.reshape(pieces, group, blk)
            out_ref[pl.ds(first, half), l, f] = rows[:half]
            out_ref[pl.ds(second, half), l, f] = rows[half:]


def join_kernel(where_ref, in_ref, out_ref):
    pieces, layers, faces, group, blk = in_ref.shape
    half = pieces // 2
    first = where_ref[0] * half
    second = half - first
    lead = where_ref[1]
    for l in range(layers):
        at = lead if l == 0 else 1 - lead
        for f in range(faces):
            low = in_ref[pl.ds(first, half), l, f].reshape(half * group, blk)
            top = in_ref[pl.ds(second, half), l, f].reshape(half * group, blk)
            out_ref[at, f] = jnp.concatenate([low.T, top.T], axis=1)


def field_of(masks, op, modes_dev):
    want = modes_dev * lax.shift_left(jnp.int32(1), jnp.maximum(op - 1, 0))
    found = jnp.int32(0)
    for j in range(masks.shape[0]):
        found = found + jnp.where(masks[j] == want, j, 0)
    return found


def prepare_kernel(
    masks_ref, adj_ref, where_ref, mean_ref, field_ref,
    dh_ref, dl_ref, hh_ref, hl_ref, ch_ref, cl_ref, dense,
):
    spot = pl.program_id(0)
    op = pl.program_id(1)
    faces, blk = mean_ref.shape[1], mean_ref.shape[2]
    lead = where_ref[1]
    layer = jnp.where(spot == 0, lead, 1 - lead)
    halo_at = pl.multiple_of((1 + layer) * blk, blk)
    cross_at = pl.multiple_of((2 - layer) * blk, blk)

    def build(src, scale):
        dense[...] = jnp.zeros_like(dense)
        for f in range(faces):
            rows = slice(f * blk, f * blk + blk)
            dense[f, rows] = src(f, 0)
            for s in range(4):
                other = adj_ref[layer, f, s]
                dense[other, rows] = dense[other, rows] + src(f, (3 + s) * blk)
        for g in range(faces):
            high, low = split2(dense[g] * scale)
            dh_ref[0, 0, :, g * blk : g * blk + blk] = high
            dl_ref[0, 0, :, g * blk : g * blk + blk] = low
        for f in range(faces):
            hh_ref[0, 0, f], hl_ref[0, 0, f] = split2(src(f, halo_at) * scale)
            ch_ref[0, 0, f], cl_ref[0, 0, f] = split2(src(f, cross_at) * scale)

    @pl.when(op == 0)
    def _():
        build(lambda f, k: mean_ref[0, f, :, pl.ds(k, blk)], 1.0)

    @pl.when(op > 0)
    def _():
        build(lambda f, k: field_ref[0, 0, f, :, pl.ds(k, blk)], COUPLING)


def off_layer(total, field, op_h, op_l, layer, f, group):
    high, low = split2(field)
    lefts, rights = [], []
    for op in range(op_h.shape[1]):
        ph, plow = permuted(high, op, group), permuted(low, op, group)
        wh, wl = op_h[layer, op, f], op_l[layer, op, f]
        lefts += [ph, plow, ph]
        rights += [wh, wh, wl]
    return total + dot_nt(jnp.concatenate(lefts, axis=1), jnp.concatenate(rights, axis=1))


def local_kernel(group, d0_ref, d1_ref, dh_ref, dl_ref, ch_ref, cl_ref, a0_ref, a1_ref):
    faces, rows, blk = d0_ref.shape
    ops = dh_ref.shape[1]
    for l, (d_ref, other_ref, acc_ref) in enumerate(
        ((d0_ref, d1_ref, a0_ref), (d1_ref, d0_ref, a1_ref))
    ):
        parts = [split2(d_ref[f]) for f in range(faces)]
        high = jnp.concatenate([p[0] for p in parts], axis=1)
        low = jnp.concatenate([p[1] for p in parts], axis=1)
        total = None
        for op in range(ops):
            ph, plow = permuted(high, op, group), permuted(low, op, group)
            term = dot_nt(ph, dh_ref[l, op]) + dot_nt(plow, dh_ref[l, op]) + dot_nt(ph, dl_ref[l, op])
            total = term if total is None else total + term
        for f in range(faces):
            here = d_ref[f] + total[:, f * blk : f * blk + blk]
            acc_ref[f] = off_layer(here, other_ref[f], ch_ref, cl_ref, l, f, group)


def finish_kernel(group, coef, layer, last, with_first, *refs):
    c_d, c_r = coef
    halo_ref, acc_ref, d_ref, r_ref = refs[:4]
    rest = list(refs[4:])
    x_ref = None if last else rest.pop(0)
    first_ref = rest.pop(0) if with_first else None
    hh_ref, hl_ref = rest[:2]
    outs = rest[2:]
    faces, rows, blk = d_ref.shape
    for f in range(faces):
        applied = off_layer(acc_ref[f], halo_ref[f], hh_ref, hl_ref, layer, f, group)
        result = r_ref[f] - applied
        if not last:
            outs[0][f] = result
            new = c_d * d_ref[f] + c_r * result
            outs[1][f] = new
            result = x_ref[f] + new
        if with_first:
            outs[-1][:, 0, f] = first_ref[f].reshape(rows // group, group, blk)
            outs[-1][:, 1, f] = result.reshape(rows // group, group, blk)
        else:
            outs[-1][f] = result


MIB = 1 << 20


def call(body, outs, args, smem=0, flops=0, limit=16):
    spaces = [pltpu.SMEM] * smem + [pltpu.VMEM] * (len(args) - smem)
    size = sum(a.size * a.dtype.itemsize for a in args) + sum(
        o.size * o.dtype.itemsize for o in outs
    )
    return pl.pallas_call(
        body,
        out_shape=outs,
        in_specs=[pl.BlockSpec(memory_space=s) for s in spaces],
        out_specs=[pl.BlockSpec(memory_space=pltpu.VMEM) for _ in outs],
        compiler_params=pltpu.CompilerParams(vmem_limit_bytes=limit * MIB),
        cost_estimate=pl.CostEstimate(flops=flops, bytes_accessed=size, transcendentals=0),
    )(*args)


def shape(dims, dtype=F32):
    return jax.ShapeDtypeStruct(tuple(dims), dtype)


def prepare(where, mean_operator, field_operators, adjacency, mode_masks, modes_dev, bits):
    layers, faces, blk, wide = mean_operator.shape
    ops = bits + 1
    full = faces * blk

    def layer_of(spot, where):
        return jnp.where(spot == 0, where[1], 1 - where[1])

    dense_spec = pl.BlockSpec((1, 1, full, full), lambda l, op, *_: (l, op, 0, 0))
    side_spec = pl.BlockSpec((1, 1, faces, blk, blk), lambda l, op, *_: (l, op, 0, 0, 0))
    grid_spec = pltpu.PrefetchScalarGridSpec(
        num_scalar_prefetch=3,
        grid=(layers, ops),
        in_specs=[
            pl.BlockSpec(
                (1, faces, blk, wide), lambda l, op, masks, adj, where: (layer_of(l, where), 0, 0, 0)
            ),
            pl.BlockSpec(
                (1, 1, faces, blk, wide),
                lambda l, op, masks, adj, where: (
                    field_of(masks, op, modes_dev), layer_of(l, where), 0, 0, 0,
                ),
            ),
        ],
        out_specs=[dense_spec] * 2 + [side_spec] * 4,
        scratch_shapes=[pltpu.VMEM((faces, full, blk), F32)],
    )
    dense = shape((layers, ops, full, full), BF16)
    side = shape((layers, ops, faces, blk, blk), BF16)
    return pl.pallas_call(
        prepare_kernel,
        grid_spec=grid_spec,
        out_shape=[dense] * 2 + [side] * 4,
        compiler_params=pltpu.CompilerParams(vmem_limit_bytes=42 * MIB),
        cost_estimate=pl.CostEstimate(flops=10**8, bytes_accessed=36 * MIB, transcendentals=0),
    )(mode_masks, adjacency, where, mean_operator, field_operators)


def pair_list(count, modes, inner):
    half = modes // 2
    pairs = []
    for s in range(count):
        t = s + 1 if (s % 2 == 0) == inner else s - 1
        if 0 <= t < count:
            turn = half if (s // 2 - t // 2) % 2 else 0
            pairs += [(s * modes + m, t * modes + (m ^ turn)) for m in range(modes)]
    return pairs


def per_device(source_field, mean_operator, field_operators, adjacency, mode_masks):
    layers, faces, blk, modes_dev = source_field.shape
    count, modes = lax.axis_size("space"), lax.axis_size("mode")
    bits = modes.bit_length() - 1
    group = modes_dev // modes
    rows = modes * group
    slab = lax.axis_index("space").astype(jnp.int32)
    flip = lax.shift_right_logical(slab, 1) & 1
    where = jnp.stack([flip, 1 - (slab & 1)])
    pieces = shape((modes, layers, faces, group, blk))
    layer = shape((faces, rows, blk))

    (sent,) = call(split_kernel, [pieces], [where, source_field], smem=1, limit=8)
    got = lax.all_to_all(sent, "mode", 0, 0, tiled=True)
    weights = prepare(
        where, mean_operator, field_operators, adjacency, mode_masks, modes_dev, bits
    )
    got, *weights = lax.optimization_barrier((got, *weights))
    dh, dl, hh, hl, ch, cl = weights
    b = [got[:, l].transpose(1, 0, 2, 3).reshape(faces, rows, blk) for l in range(layers)]

    links = [pair_list(count, modes, True), pair_list(count, modes, False)]
    sigma = THETA / DELTA
    rho = 1.0 / sigma
    d, r = [v / THETA for v in b], b
    x = d
    flops = 2 * rows * blk * blk * 3 * (bits + 1) * faces
    for step in range(DEGREE):
        last = step == DEGREE - 1
        halo = [lax.ppermute(d[l], AXES, links[l]) for l in range(layers)]
        acc = call(
            functools.partial(local_kernel, group),
            [layer, layer],
            [*d, dh, dl, ch, cl],
            flops=10 * flops,
        )
        rho_new = 1.0 / (2.0 * sigma - rho)
        coef = (rho_new * rho, 2.0 * rho_new / DELTA)
        rho = rho_new
        fresh = []
        for l in range(layers):
            gather = l == layers - 1 and step >= DEGREE - 2
            args = [halo[l], acc[l], d[l], r[l]] + ([] if last else [x[l]])
            args += [fresh[0][-1]] if gather else []
            fresh.append(
                call(
                    functools.partial(finish_kernel, group, coef, l, last, gather),
                    [layer] * (0 if last else 2) + [pieces if gather else layer],
                    args + [hh, hl],
                    flops=2 * flops,
                )
            )
        if last:
            r_back = lax.all_to_all(fresh[-1][-1], "mode", 0, 0, tiled=True)
        else:
            r, d, x = zip(*fresh)
            if step == DEGREE - 2:
                x_back = lax.all_to_all(x[-1], "mode", 0, 0, tiled=True)
    field = shape(source_field.shape)
    (x_end,) = call(join_kernel, [field], [where, x_back], smem=1, limit=8)
    (r_end,) = call(join_kernel, [field], [where, r_back], smem=1, limit=8)
    return x_end, r_end


def solution(mesh):
    in_specs = (
        P("space", None, None, "mode"),
        P("space", None, None, None),
        P(None, "space", None, None, None),
        P("space", None, None),
        P(),
    )
    out_specs = (P("space", None, None, "mode"), P("space", None, None, "mode"))
    return jax.shard_map(
        per_device, mesh=mesh, in_specs=in_specs, out_specs=out_specs, check_vma=False
    )
```

```python
import functools

import jax
import jax.numpy as jnp
from jax import lax
from jax.experimental import pallas as pl
from jax.experimental.pallas import tpu as pltpu
from jax.sharding import PartitionSpec as P

DEGREE = 4
COUPLING = 0.5773502691896258
THETA = 1.0
DELTA = 0.7
AXES = ("space", "mode")
F32 = jnp.float32
BF16 = jnp.bfloat16
NT = (((1,), (1,)), ((), ()))


def split2(value):
    high = value.astype(BF16)
    return high, (value - high.astype(F32)).astype(BF16)


def dot_nt(left, right):
    return lax.dot_general(left, right, NT, preferred_element_type=F32)


def swap_rows(value, bit, group):
    step = group << bit
    count = value.shape[0] // step
    return jnp.concatenate(
        [value[(i ^ 1) * step : (i ^ 1) * step + step] for i in range(count)], axis=0
    )


def permuted(value, op, group):
    return value if op == 0 else swap_rows(value, op - 1, group)


def split_kernel(where_ref, field_ref, out_ref):
    pieces, _, faces, group, blk = out_ref.shape
    half = pieces // 2
    first = where_ref[0] * half
    second = half - first
    for f in range(faces):
        rows = field_ref[0, f].T.reshape(pieces, group, blk)
        out_ref[pl.ds(first, half), 0, f] = rows[:half]
        out_ref[pl.ds(second, half), 0, f] = rows[half:]


def join_kernel(where_ref, in_ref, x_ref, r_ref, buffer, sems):
    pieces, fields, layers, faces, group, blk = in_ref.shape
    half = pieces // 2
    first = where_ref[0] * half
    second = half - first
    lead = where_ref[1]
    copies = []
    for k, out_ref in enumerate((x_ref, r_ref)):
        for l in range(layers):
            at = lead if l == 0 else 1 - lead
            for f in range(faces):
                low = in_ref[pl.ds(first, half), k, l, f].reshape(half * group, blk)
                top = in_ref[pl.ds(second, half), k, l, f].reshape(half * group, blk)
                buffer[k, l, f] = jnp.concatenate([low.T, top.T], axis=1)
            copies.append(pltpu.make_async_copy(buffer.at[k, l], out_ref.at[at], sems.at[k, l]))
            copies[-1].start()
    for copy in copies:
        copy.wait()


def field_of(masks, op, modes_dev):
    want = modes_dev * lax.shift_left(jnp.int32(1), jnp.maximum(op - 1, 0))
    found = jnp.int32(0)
    for j in range(masks.shape[0]):
        found = found + jnp.where(masks[j] == want, j, 0)
    return found


def prepare_kernel(
    masks_ref, adj_ref, where_ref, mean_ref, field_ref,
    dh_ref, dl_ref, hh_ref, hl_ref, ch_ref, cl_ref, dense,
):
    spot = pl.program_id(0)
    op = pl.program_id(1)
    faces, blk = mean_ref.shape[1], mean_ref.shape[2]
    lead = where_ref[1]
    layer = jnp.where(spot == 0, lead, 1 - lead)
    halo_at = pl.multiple_of((1 + layer) * blk, blk)
    cross_at = pl.multiple_of((2 - layer) * blk, blk)

    def build(src, scale):
        dense[...] = jnp.zeros_like(dense)
        for f in range(faces):
            rows = slice(f * blk, f * blk + blk)
            dense[f, rows] = src(f, 0)
            for s in range(4):
                other = adj_ref[layer, f, s]
                dense[other, rows] = dense[other, rows] + src(f, (3 + s) * blk)
        for g in range(faces):
            high, low = split2(dense[g] * scale)
            dh_ref[0, 0, :, g * blk : g * blk + blk] = high
            dl_ref[0, 0, :, g * blk : g * blk + blk] = low
        for f in range(faces):
            hh_ref[0, 0, f], hl_ref[0, 0, f] = split2(src(f, halo_at) * scale)
            ch_ref[0, 0, f], cl_ref[0, 0, f] = split2(src(f, cross_at) * scale)

    @pl.when(op == 0)
    def _():
        build(lambda f, k: mean_ref[0, f, :, pl.ds(k, blk)], 1.0)

    @pl.when(op > 0)
    def _():
        build(lambda f, k: field_ref[0, 0, f, :, pl.ds(k, blk)], COUPLING)


def off_layer(total, field, op_h, op_l, layer, f, group):
    high, low = split2(field)
    lefts, rights = [], []
    for op in range(op_h.shape[1]):
        ph, plow = permuted(high, op, group), permuted(low, op, group)
        wh, wl = op_h[layer, op, f], op_l[layer, op, f]
        lefts += [ph, plow, ph]
        rights += [wh, wh, wl]
    return total + dot_nt(jnp.concatenate(lefts, axis=1), jnp.concatenate(rights, axis=1))


def local_kernel(group, with_x, *refs):
    count = 6 if with_x else 4
    d_refs, r_refs, x_refs = refs[0:2], refs[2:4], refs[4:count]
    dh_ref, dl_ref, ch_ref, cl_ref = refs[count : count + 4]
    pre_refs = refs[count + 4 : count + 6]
    x_outs = refs[count + 6 :]
    faces, rows, blk = d_refs[0].shape
    ops = dh_ref.shape[1]
    for l in range(2):
        parts = [split2(d_refs[l][f]) for f in range(faces)]
        high = jnp.concatenate([p[0] for p in parts], axis=1)
        low = jnp.concatenate([p[1] for p in parts], axis=1)
        total = None
        for op in range(ops):
            ph, plow = permuted(high, op, group), permuted(low, op, group)
            term = dot_nt(ph, dh_ref[l, op]) + dot_nt(plow, dh_ref[l, op]) + dot_nt(ph, dl_ref[l, op])
            total = term if total is None else total + term
        for f in range(faces):
            here = d_refs[l][f] + total[:, f * blk : f * blk + blk]
            applied = off_layer(here, d_refs[1 - l][f], ch_ref, cl_ref, l, f, group)
            pre_refs[l][f] = r_refs[l][f] - applied
            if with_x:
                x_outs[l][f] = x_refs[l][f] + d_refs[l][f]


def finish_kernel(group, coef, layer, halo_ref, pre_ref, hh_ref, hl_ref, d_ref, r_out, d_out):
    c_d, c_r = coef
    for f in range(halo_ref.shape[0]):
        residual = pre_ref[f] - off_layer(0.0, halo_ref[f], hh_ref, hl_ref, layer, f, group)
        r_out[f] = residual
        d_out[f] = c_d * d_ref[f] + c_r * residual


def last_kernel(
    group, halo0_ref, halo1_ref, pre0_ref, pre1_ref, x0_ref, x1_ref, hh_ref, hl_ref,
    send_ref, buffer, sems,
):
    copies = []

    def send(k, l):
        copies.append(
            pltpu.make_async_copy(buffer.at[:, k, l], send_ref.at[:, k, l], sems.at[k, l])
        )
        copies[-1].start()

    faces, _, blk = halo0_ref.shape
    for l, x_ref in enumerate((x0_ref, x1_ref)):
        for f in range(faces):
            buffer[:, 0, l, f] = x_ref[f].reshape(-1, group, blk)
        send(0, l)
    for l, (halo_ref, pre_ref) in enumerate(((halo0_ref, pre0_ref), (halo1_ref, pre1_ref))):
        for f in range(faces):
            share = off_layer(0.0, halo_ref[f], hh_ref, hl_ref, l, f, group)
            buffer[:, 1, l, f] = (pre_ref[f] - share).reshape(-1, group, blk)
        send(1, l)
    for copy in copies:
        copy.wait()


MIB = 1 << 20


def call(body, outs, args, smem=0, flops=0, limit=6, out_space=pltpu.VMEM, scratch=()):
    spaces = [pltpu.SMEM] * smem + [pltpu.VMEM] * (len(args) - smem)
    size = sum(a.size * a.dtype.itemsize for a in args) + sum(
        o.size * o.dtype.itemsize for o in outs
    )
    return pl.pallas_call(
        body,
        out_shape=outs,
        in_specs=[pl.BlockSpec(memory_space=s) for s in spaces],
        out_specs=[pl.BlockSpec(memory_space=out_space) for _ in outs],
        scratch_shapes=list(scratch),
        compiler_params=pltpu.CompilerParams(vmem_limit_bytes=limit * MIB),
        cost_estimate=pl.CostEstimate(flops=flops, bytes_accessed=size, transcendentals=0),
    )(*args)


def shape(dims, dtype=F32):
    return jax.ShapeDtypeStruct(tuple(dims), dtype)


def prepare(where, mean_operator, field_operators, adjacency, mode_masks, modes_dev, bits):
    layers, faces, blk, wide = mean_operator.shape
    ops = bits + 1
    full = faces * blk

    def layer_of(spot, where):
        return jnp.where(spot == 0, where[1], 1 - where[1])

    dense_spec = pl.BlockSpec((1, 1, full, full), lambda l, op, *_: (l, op, 0, 0))
    side_spec = pl.BlockSpec((1, 1, faces, blk, blk), lambda l, op, *_: (l, op, 0, 0, 0))
    grid_spec = pltpu.PrefetchScalarGridSpec(
        num_scalar_prefetch=3,
        grid=(layers, ops),
        in_specs=[
            pl.BlockSpec(
                (1, faces, blk, wide), lambda l, op, masks, adj, where: (layer_of(l, where), 0, 0, 0)
            ),
            pl.BlockSpec(
                (1, 1, faces, blk, wide),
                lambda l, op, masks, adj, where: (
                    field_of(masks, op, modes_dev), layer_of(l, where), 0, 0, 0,
                ),
            ),
        ],
        out_specs=[dense_spec] * 2 + [side_spec] * 4,
        scratch_shapes=[pltpu.VMEM((faces, full, blk), F32)],
    )
    dense = shape((layers, ops, full, full), BF16)
    side = shape((layers, ops, faces, blk, blk), BF16)
    return pl.pallas_call(
        prepare_kernel,
        grid_spec=grid_spec,
        out_shape=[dense] * 2 + [side] * 4,
        compiler_params=pltpu.CompilerParams(vmem_limit_bytes=56 * MIB),
        cost_estimate=pl.CostEstimate(flops=10**8, bytes_accessed=36 * MIB, transcendentals=0),
    )(mode_masks, adjacency, where, mean_operator, field_operators)


def pair_list(count, modes, inner):
    half = modes // 2
    pairs = []
    for s in range(count):
        t = s + 1 if (s % 2 == 0) == inner else s - 1
        if 0 <= t < count:
            turn = half if (s // 2 - t // 2) % 2 else 0
            pairs += [(s * modes + m, t * modes + (m ^ turn)) for m in range(modes)]
    return pairs


def per_device(source_field, mean_operator, field_operators, adjacency, mode_masks):
    layers, faces, blk, modes_dev = source_field.shape
    count, modes = lax.axis_size("space"), lax.axis_size("mode")
    bits = modes.bit_length() - 1
    group = modes_dev // modes
    rows = modes * group
    slab = lax.axis_index("space").astype(jnp.int32)
    flip = lax.shift_right_logical(slab, 1) & 1
    where = jnp.stack([flip, 1 - (slab & 1)])
    pieces = shape((modes, layers, faces, group, blk))
    layer = shape((faces, rows, blk))

    sent = pl.pallas_call(
        split_kernel,
        grid_spec=pltpu.PrefetchScalarGridSpec(
            num_scalar_prefetch=1,
            grid=(layers,),
            in_specs=[
                pl.BlockSpec(
                    (1, faces, blk, modes_dev),
                    lambda l, where: (jnp.where(l == 0, where[1], 1 - where[1]), 0, 0, 0),
                )
            ],
            out_specs=pl.BlockSpec((modes, 1, faces, group, blk), lambda l, where: (0, l, 0, 0, 0)),
        ),
        out_shape=pieces,
        compiler_params=pltpu.CompilerParams(vmem_limit_bytes=60 * MIB),
        cost_estimate=pl.CostEstimate(flops=0, bytes_accessed=2 * MIB, transcendentals=0),
    )(where, source_field)
    got = lax.all_to_all(sent, "mode", 0, 0, tiled=True)
    weights = prepare(
        where, mean_operator, field_operators, adjacency, mode_masks, modes_dev, bits
    )
    got, *weights = lax.optimization_barrier((got, *weights))
    dh, dl, hh, hl, ch, cl = weights
    b = [got[:, l].transpose(1, 0, 2, 3).reshape(faces, rows, blk) for l in range(layers)]

    links = [pair_list(count, modes, True), pair_list(count, modes, False)]
    sigma = THETA / DELTA
    rho = 1.0 / sigma
    d, r = [v / THETA for v in b], b
    flops = 2 * rows * blk * blk * 3 * (bits + 1) * faces
    for step in range(DEGREE):
        last = step == DEGREE - 1
        halo = [lax.ppermute(d[l], AXES, links[l]) for l in range(layers)]
        pre0, pre1, *x_next = call(
            functools.partial(local_kernel, group, step > 0),
            [layer] * (4 if step else 2),
            [*d, *r, *(x if step else []), dh, dl, ch, cl],
            flops=10 * flops,
        )
        pre = [pre0, pre1]
        x = x_next if step else d
        rho_new = 1.0 / (2.0 * sigma - rho)
        coef = (rho_new * rho, 2.0 * rho_new / DELTA)
        rho = rho_new
        if not last:
            fresh = []
            for l in range(layers):
                if fresh:
                    pre[l], _ = lax.optimization_barrier((pre[l], fresh[0][1]))
                fresh.append(
                    call(
                        functools.partial(finish_kernel, group, coef, l),
                        [layer, layer],
                        [halo[l], pre[l], hh, hl, d[l]],
                        flops=2 * flops,
                    )
                )
            r, d = zip(*fresh)
    both = (modes, 2) + pieces.shape[1:]
    (send,) = call(
        functools.partial(last_kernel, group),
        [shape(both)],
        [*halo, *pre, *x, hh, hl],
        flops=4 * flops,
        limit=12,
        out_space=pltpu.HBM,
        scratch=[pltpu.VMEM(both, F32), pltpu.SemaphoreType.DMA((2, layers))],
    )
    back = lax.all_to_all(send, "mode", 0, 0, tiled=True)
    field = shape(source_field.shape)
    return tuple(
        call(
            join_kernel,
            [field, field],
            [where, back],
            smem=1,
            limit=12,
            out_space=pltpu.HBM,
            scratch=[
                pltpu.VMEM((2,) + source_field.shape, F32),
                pltpu.SemaphoreType.DMA((2, layers)),
            ],
        )
    )


def solution(mesh):
    in_specs = (
        P("space", None, None, "mode"),
        P("space", None, None, None),
        P(None, "space", None, None, None),
        P("space", None, None),
        P(),
    )
    out_specs = (P("space", None, None, "mode"), P("space", None, None, "mode"))
    return jax.shard_map(
        per_device, mesh=mesh, in_specs=in_specs, out_specs=out_specs, check_vma=False
    )
```

```python
import functools

import jax
import jax.numpy as jnp
from jax import lax
from jax.experimental import pallas as pl
from jax.experimental.pallas import tpu as pltpu
from jax.sharding import PartitionSpec as P

DEGREE = 4
COUPLING = 0.5773502691896258
THETA = 1.0
DELTA = 0.7
AXES = ("space", "mode")
F32 = jnp.float32
BF16 = jnp.bfloat16
NT = (((1,), (1,)), ((), ()))


def split2(value):
    high = value.astype(BF16)
    return high, (value - high.astype(F32)).astype(BF16)


def dot_nt(left, right):
    return lax.dot_general(left, right, NT, preferred_element_type=F32)


def swap_rows(value, bit, group):
    step = group << bit
    count = value.shape[0] // step
    return jnp.concatenate(
        [value[(i ^ 1) * step : (i ^ 1) * step + step] for i in range(count)], axis=0
    )


def permuted(value, op, group):
    return value if op == 0 else swap_rows(value, op - 1, group)


def place():
    slab = lax.axis_index("space").astype(jnp.int32)
    return lax.shift_right_logical(slab, 1) & 1, 1 - (slab & 1)


def split_kernel(field_ref, out_ref, arrived, laid, in_sems, out_sems):
    pieces, layers, faces, group, blk = out_ref.shape
    half = pieces // 2
    flip, lead = place()
    first = flip * half
    second = half - first
    ins, outs = [], []
    for l in range(layers):
        at = lead if l == 0 else 1 - lead
        for f in range(faces):
            ins.append(
                pltpu.make_async_copy(field_ref.at[at, f], arrived.at[l, f], in_sems.at[l, f])
            )
            ins[-1].start()
    for l in range(layers):
        for f in range(faces):
            ins[l * faces + f].wait()
            rows = arrived[l, f].T.reshape(pieces, group, blk)
            laid[pl.ds(first, half), l, f] = rows[:half]
            laid[pl.ds(second, half), l, f] = rows[half:]
        outs.append(pltpu.make_async_copy(laid.at[:, l], out_ref.at[:, l], out_sems.at[l]))
        outs[-1].start()
    for copy in outs:
        copy.wait()


def join_kernel(in_ref, x_ref, r_ref, buffer, sems):
    pieces, fields, layers, faces, group, blk = in_ref.shape
    half = pieces // 2
    flip, lead = place()
    first = flip * half
    second = half - first
    copies = []
    for k, out_ref in enumerate((x_ref, r_ref)):
        for l in range(layers):
            at = lead if l == 0 else 1 - lead
            for f in range(faces):
                low = in_ref[pl.ds(first, half), k, l, f].reshape(half * group, blk)
                top = in_ref[pl.ds(second, half), k, l, f].reshape(half * group, blk)
                buffer[k, l, f] = jnp.concatenate([low.T, top.T], axis=1)
            copies.append(pltpu.make_async_copy(buffer.at[k, l], out_ref.at[at], sems.at[k, l]))
            copies[-1].start()
    for copy in copies:
        copy.wait()


def field_of(masks, op, modes_dev):
    want = modes_dev * lax.shift_left(jnp.int32(1), jnp.maximum(op - 1, 0))
    found = jnp.int32(0)
    for j in range(masks.shape[0]):
        found = found + jnp.where(masks[j] == want, j, 0)
    return found


def prepare_kernel(
    masks_ref, adj_ref, mean_ref, field_ref,
    dh_ref, dl_ref, hh_ref, hl_ref, ch_ref, cl_ref, dense,
):
    spot = pl.program_id(0)
    op = pl.program_id(1)
    faces, blk = mean_ref.shape[1], mean_ref.shape[2]
    lead = place()[1]
    layer = jnp.where(spot == 0, lead, 1 - lead)
    halo_at = pl.multiple_of((1 + layer) * blk, blk)
    cross_at = pl.multiple_of((2 - layer) * blk, blk)

    def build(src, scale):
        dense[...] = jnp.zeros_like(dense)
        for f in range(faces):
            rows = slice(f * blk, f * blk + blk)
            dense[f, rows] = src(f, 0)
            for s in range(4):
                other = adj_ref[layer, f, s]
                dense[other, rows] = dense[other, rows] + src(f, (3 + s) * blk)
        for g in range(faces):
            high, low = split2(dense[g] * scale)
            dh_ref[0, 0, :, g * blk : g * blk + blk] = high
            dl_ref[0, 0, :, g * blk : g * blk + blk] = low
        for f in range(faces):
            hh_ref[0, 0, f], hl_ref[0, 0, f] = split2(src(f, halo_at) * scale)
            ch_ref[0, 0, f], cl_ref[0, 0, f] = split2(src(f, cross_at) * scale)

    @pl.when(op == 0)
    def _():
        build(lambda f, k: mean_ref[0, f, :, pl.ds(k, blk)], 1.0)

    @pl.when(op > 0)
    def _():
        build(lambda f, k: field_ref[0, 0, f, :, pl.ds(k, blk)], COUPLING)


def off_layer(total, field, op_h, op_l, layer, f, group):
    high, low = split2(field)
    lefts, rights = [], []
    for op in range(op_h.shape[1]):
        ph, plow = permuted(high, op, group), permuted(low, op, group)
        wh, wl = op_h[layer, op, f], op_l[layer, op, f]
        lefts += [ph, plow, ph]
        rights += [wh, wh, wl]
    return total + dot_nt(jnp.concatenate(lefts, axis=1), jnp.concatenate(rights, axis=1))


def local_kernel(group, with_x, *refs):
    count = 6 if with_x else 4
    d_refs, r_refs, x_refs = refs[0:2], refs[2:4], refs[4:count]
    dh_ref, dl_ref, ch_ref, cl_ref = refs[count : count + 4]
    pre_refs = refs[count + 4 : count + 6]
    x_outs = refs[count + 6 :]
    faces, rows, blk = d_refs[0].shape
    ops = dh_ref.shape[1]
    for l in range(2):
        parts = [split2(d_refs[l][f]) for f in range(faces)]
        high = jnp.concatenate([p[0] for p in parts], axis=1)
        low = jnp.concatenate([p[1] for p in parts], axis=1)
        total = None
        for op in range(ops):
            ph, plow = permuted(high, op, group), permuted(low, op, group)
            term = dot_nt(ph, dh_ref[l, op]) + dot_nt(plow, dh_ref[l, op]) + dot_nt(ph, dl_ref[l, op])
            total = term if total is None else total + term
        for f in range(faces):
            here = d_refs[l][f] + total[:, f * blk : f * blk + blk]
            applied = off_layer(here, d_refs[1 - l][f], ch_ref, cl_ref, l, f, group)
            pre_refs[l][f] = r_refs[l][f] - applied
            if with_x:
                x_outs[l][f] = x_refs[l][f] + d_refs[l][f]


def finish_kernel(group, coef, layer, halo_ref, pre_ref, hh_ref, hl_ref, *rest):
    for f in range(halo_ref.shape[0]):
        residual = pre_ref[f] - off_layer(0.0, halo_ref[f], hh_ref, hl_ref, layer, f, group)
        if coef is None:
            rest[0][f] = residual
        else:
            d_ref, r_out, d_out = rest
            r_out[f] = residual
            d_out[f] = coef[0] * d_ref[f] + coef[1] * residual


def last_kernel(
    group, halo_ref, pre_ref, r0_ref, x0_ref, x1_ref, hh_ref, hl_ref, send_ref, buffer, sems
):
    copies = []

    def send(k, l, value):
        for f in range(halo_ref.shape[0]):
            buffer[:, k, l, f] = value(f).reshape(-1, group, value(f).shape[-1])
        copies.append(
            pltpu.make_async_copy(buffer.at[:, k, l], send_ref.at[:, k, l], sems.at[k, l])
        )
        copies[-1].start()

    send(0, 0, lambda f: x0_ref[f])
    send(0, 1, lambda f: x1_ref[f])
    send(1, 0, lambda f: r0_ref[f])
    ends = [
        pre_ref[f] - off_layer(0.0, halo_ref[f], hh_ref, hl_ref, 1, f, group)
        for f in range(halo_ref.shape[0])
    ]
    send(1, 1, lambda f: ends[f])
    for copy in copies:
        copy.wait()


MIB = 1 << 20


def call(
    body, outs, args, flops=0, limit=6, in_space=pltpu.VMEM, out_space=pltpu.VMEM, scratch=()
):
    size = sum(a.size * a.dtype.itemsize for a in args) + sum(
        o.size * o.dtype.itemsize for o in outs
    )
    return pl.pallas_call(
        body,
        out_shape=outs,
        in_specs=[pl.BlockSpec(memory_space=in_space) for _ in args],
        out_specs=[pl.BlockSpec(memory_space=out_space) for _ in outs],
        scratch_shapes=list(scratch),
        compiler_params=pltpu.CompilerParams(vmem_limit_bytes=limit * MIB),
        cost_estimate=pl.CostEstimate(flops=flops, bytes_accessed=size, transcendentals=0),
    )(*args)


def shape(dims, dtype=F32):
    return jax.ShapeDtypeStruct(tuple(dims), dtype)


def prepare(mean_operator, field_operators, adjacency, mode_masks, modes_dev, bits):
    layers, faces, blk, wide = mean_operator.shape
    ops = bits + 1
    full = faces * blk

    def layer_of(spot):
        lead = place()[1]
        return jnp.where(spot == 0, lead, 1 - lead)

    dense_spec = pl.BlockSpec((1, 1, full, full), lambda l, op, *_: (l, op, 0, 0))
    side_spec = pl.BlockSpec((1, 1, faces, blk, blk), lambda l, op, *_: (l, op, 0, 0, 0))
    grid_spec = pltpu.PrefetchScalarGridSpec(
        num_scalar_prefetch=2,
        grid=(layers, ops),
        in_specs=[
            pl.BlockSpec(
                (1, faces, blk, wide), lambda l, op, masks, adj: (layer_of(l), 0, 0, 0)
            ),
            pl.BlockSpec(
                (1, 1, faces, blk, wide),
                lambda l, op, masks, adj: (field_of(masks, op, modes_dev), layer_of(l), 0, 0, 0),
            ),
        ],
        out_specs=[dense_spec] * 2 + [side_spec] * 4,
        scratch_shapes=[pltpu.VMEM((faces, full, blk), F32)],
    )
    dense = shape((layers, ops, full, full), BF16)
    side = shape((layers, ops, faces, blk, blk), BF16)
    return pl.pallas_call(
        prepare_kernel,
        grid_spec=grid_spec,
        out_shape=[dense] * 2 + [side] * 4,
        compiler_params=pltpu.CompilerParams(vmem_limit_bytes=56 * MIB),
        cost_estimate=pl.CostEstimate(flops=10**8, bytes_accessed=36 * MIB, transcendentals=0),
    )(mode_masks, adjacency, mean_operator, field_operators)


def pair_list(count, modes, inner):
    half = modes // 2
    pairs = []
    for s in range(count):
        t = s + 1 if (s % 2 == 0) == inner else s - 1
        if 0 <= t < count:
            turn = half if (s // 2 - t // 2) % 2 else 0
            pairs += [(s * modes + m, t * modes + (m ^ turn)) for m in range(modes)]
    return pairs


def per_device(source_field, mean_operator, field_operators, adjacency, mode_masks):
    layers, faces, blk, modes_dev = source_field.shape
    count, modes = lax.axis_size("space"), lax.axis_size("mode")
    bits = modes.bit_length() - 1
    group = modes_dev // modes
    rows = modes * group
    pieces = shape((modes, layers, faces, group, blk))
    layer = shape((faces, rows, blk))

    (sent,) = call(
        split_kernel,
        [pieces],
        [source_field],
        limit=60,
        in_space=pltpu.HBM,
        out_space=pltpu.HBM,
        scratch=[
            pltpu.VMEM(source_field.shape, F32),
            pltpu.VMEM(pieces.shape, F32),
            pltpu.SemaphoreType.DMA((layers, faces)),
            pltpu.SemaphoreType.DMA((layers,)),
        ],
    )
    got = lax.all_to_all(sent, "mode", 0, 0, tiled=True)
    weights = prepare(
        mean_operator, field_operators, adjacency, mode_masks, modes_dev, bits
    )
    got, *weights = lax.optimization_barrier((got, *weights))
    dh, dl, hh, hl, ch, cl = weights
    b = [got[:, l].transpose(1, 0, 2, 3).reshape(faces, rows, blk) for l in range(layers)]

    links = [pair_list(count, modes, True), pair_list(count, modes, False)]
    sigma = THETA / DELTA
    rho = 1.0 / sigma
    d, r = [v / THETA for v in b], b
    flops = 2 * rows * blk * blk * 3 * (bits + 1) * faces
    for step in range(DEGREE):
        last = step == DEGREE - 1
        halo = [lax.ppermute(d[l], AXES, links[l]) for l in range(layers)]
        pre0, pre1, *x_next = call(
            functools.partial(local_kernel, group, step > 0),
            [layer] * (4 if step else 2),
            [*d, *r, *(x if step else []), dh, dl, ch, cl],
        )
        pre = [pre0, pre1]
        x = x_next if step else d
        rho_new = 1.0 / (2.0 * sigma - rho)
        coef = (rho_new * rho, 2.0 * rho_new / DELTA)
        rho = rho_new
        if not last:
            fresh = []
            for l in range(layers):
                if fresh:
                    pre[l], _ = lax.optimization_barrier((pre[l], fresh[0][1]))
                fresh.append(
                    call(
                        functools.partial(finish_kernel, group, coef, l),
                        [layer, layer],
                        [halo[l], pre[l], hh, hl, d[l]],
                    )
                )
            r, d = zip(*fresh)
    (r_end,) = call(
        functools.partial(finish_kernel, group, None, 0), [layer], [halo[0], pre[0], hh, hl]
    )
    both = (modes, 2) + pieces.shape[1:]
    (send,) = call(
        functools.partial(last_kernel, group),
        [shape(both)],
        [halo[1], pre[1], r_end, *x, hh, hl],
        limit=12,
        out_space=pltpu.HBM,
        scratch=[pltpu.VMEM(both, F32), pltpu.SemaphoreType.DMA((2, layers))],
    )
    back = lax.all_to_all(send, "mode", 0, 0, tiled=True)
    field = shape(source_field.shape)
    return tuple(
        call(
            join_kernel,
            [field, field],
            [back],
            limit=12,
            out_space=pltpu.HBM,
            scratch=[
                pltpu.VMEM((2,) + source_field.shape, F32),
                pltpu.SemaphoreType.DMA((2, layers)),
            ],
        )
    )


def solution(mesh):
    in_specs = (
        P("space", None, None, "mode"),
        P("space", None, None, None),
        P(None, "space", None, None, None),
        P("space", None, None),
        P(),
    )
    out_specs = (P("space", None, None, "mode"), P("space", None, None, "mode"))
    return jax.shard_map(
        per_device, mesh=mesh, in_specs=in_specs, out_specs=out_specs, check_vma=False
    )
```

```python
import functools

import jax
import jax.numpy as jnp
from jax import lax
from jax.experimental import pallas as pl
from jax.experimental.pallas import tpu as pltpu
from jax.sharding import PartitionSpec as P

DEGREE = 4
COUPLING = 0.5773502691896258
THETA = 1.0
DELTA = 0.7
AXES = ("space", "mode")
F32 = jnp.float32
BF16 = jnp.bfloat16
NT = (((1,), (1,)), ((), ()))


def split2(value):
    high = value.astype(BF16)
    return high, (value - high.astype(F32)).astype(BF16)


def dot_nt(left, right):
    return lax.dot_general(left, right, NT, preferred_element_type=F32)


def swap_rows(value, bit, group):
    step = group << bit
    count = value.shape[0] // step
    return jnp.concatenate(
        [value[(i ^ 1) * step : (i ^ 1) * step + step] for i in range(count)], axis=0
    )


def permuted(value, op, group):
    return value if op == 0 else swap_rows(value, op - 1, group)


def place():
    slab = lax.axis_index("space").astype(jnp.int32)
    return lax.shift_right_logical(slab, 1) & 1, 1 - (slab & 1)


def split_kernel(field_ref, out_ref, arrived, laid, in_sems, out_sems):
    pieces, layers, faces, group, blk = out_ref.shape
    half = pieces // 2
    flip, lead = place()
    first = flip * half
    second = half - first
    ins, outs = [], []
    for l in range(layers):
        at = lead if l == 0 else 1 - lead
        for f in range(faces):
            ins.append(
                pltpu.make_async_copy(field_ref.at[at, f], arrived.at[l, f], in_sems.at[l, f])
            )
            ins[-1].start()
    for l in range(layers):
        for f in range(faces):
            ins[l * faces + f].wait()
            rows = arrived[l, f].T.reshape(pieces, group, blk)
            laid[pl.ds(first, half), l, f] = rows[:half]
            laid[pl.ds(second, half), l, f] = rows[half:]
        outs.append(pltpu.make_async_copy(laid.at[:, l], out_ref.at[:, l], out_sems.at[l]))
        outs[-1].start()
    for copy in outs:
        copy.wait()


def join_kernel(in_ref, x_ref, r_ref, buffer, sems):
    pieces, fields, layers, faces, group, blk = in_ref.shape
    half = pieces // 2
    flip, lead = place()
    first = flip * half
    second = half - first
    copies = []
    for k, out_ref in enumerate((x_ref, r_ref)):
        for l in range(layers):
            at = lead if l == 0 else 1 - lead
            for f in range(faces):
                low = in_ref[pl.ds(first, half), k, l, f].reshape(half * group, blk)
                top = in_ref[pl.ds(second, half), k, l, f].reshape(half * group, blk)
                buffer[k, l, f] = jnp.concatenate([low.T, top.T], axis=1)
            copies.append(pltpu.make_async_copy(buffer.at[k, l], out_ref.at[at], sems.at[k, l]))
            copies[-1].start()
    for copy in copies:
        copy.wait()


def field_of(masks, op, modes_dev):
    want = modes_dev * lax.shift_left(jnp.int32(1), jnp.maximum(op - 1, 0))
    found = jnp.int32(0)
    for j in range(masks.shape[0]):
        found = found + jnp.where(masks[j] == want, j, 0)
    return found


def prepare_kernel(
    masks_ref, adj_ref, mean_ref, field_ref,
    dh_ref, dl_ref, hh_ref, hl_ref, ch_ref, cl_ref, dense,
):
    spot = pl.program_id(0)
    op = pl.program_id(1)
    faces, blk = mean_ref.shape[1], mean_ref.shape[2]
    lead = place()[1]
    layer = jnp.where(spot == 0, lead, 1 - lead)
    halo_at = pl.multiple_of((1 + layer) * blk, blk)
    cross_at = pl.multiple_of((2 - layer) * blk, blk)
    slab = lax.axis_index("space").astype(jnp.int32)
    ends = (slab == 0) | (slab == lax.axis_size("space") - 1)
    inside = jnp.where((spot == 1) & ends, 0.0, 1.0).astype(F32)

    def build(src, scale):
        dense[...] = jnp.zeros_like(dense)
        for f in range(faces):
            rows = slice(f * blk, f * blk + blk)
            dense[f, rows] = src(f, 0)
            for s in range(4):
                other = adj_ref[layer, f, s]
                dense[other, rows] = dense[other, rows] + src(f, (3 + s) * blk)
        for g in range(faces):
            high, low = split2(dense[g] * scale)
            dh_ref[0, 0, :, g * blk : g * blk + blk] = high
            dl_ref[0, 0, :, g * blk : g * blk + blk] = low
        for f in range(faces):
            hh_ref[0, 0, f], hl_ref[0, 0, f] = split2(src(f, halo_at) * scale * inside)
            ch_ref[0, 0, f], cl_ref[0, 0, f] = split2(src(f, cross_at) * scale)

    @pl.when(op == 0)
    def _():
        build(lambda f, k: mean_ref[0, f, :, pl.ds(k, blk)], 1.0)

    @pl.when(op > 0)
    def _():
        build(lambda f, k: field_ref[0, 0, f, :, pl.ds(k, blk)], COUPLING)


def off_layer(total, field, op_h, op_l, layer, f, group):
    high, low = split2(field)
    ops = range(op_h.shape[1])
    heavy = [op_h[layer, op, f] for op in ops]
    wide = [jnp.concatenate([op_h[layer, op, f], op_l[layer, op, f]], axis=0) for op in ops]
    tops = jnp.concatenate([permuted(high, op, group) for op in ops], axis=1)
    rest = jnp.concatenate([permuted(low, op, group) for op in ops], axis=1)
    both = dot_nt(tops, jnp.concatenate(wide, axis=1))
    blk = field.shape[1]
    small = both[:, blk:] + dot_nt(rest, jnp.concatenate(heavy, axis=1))
    return total + (both[:, :blk] + small)


def local_kernel(group, with_x, *refs):
    count = 6 if with_x else 4
    d_refs, r_refs, x_refs = refs[0:2], refs[2:4], refs[4:count]
    dh_ref, dl_ref, ch_ref, cl_ref = refs[count : count + 4]
    pre_refs = refs[count + 4 : count + 6]
    x_outs = refs[count + 6 :]
    faces, rows, blk = d_refs[0].shape
    ops = dh_ref.shape[1]
    for l in range(2):
        parts = [split2(d_refs[l][f]) for f in range(faces)]
        high = jnp.concatenate([p[0] for p in parts], axis=1)
        low = jnp.concatenate([p[1] for p in parts], axis=1)
        total = None
        for op in range(ops):
            ph, plow = permuted(high, op, group), permuted(low, op, group)
            term = dot_nt(ph, dh_ref[l, op]) + dot_nt(plow, dh_ref[l, op]) + dot_nt(ph, dl_ref[l, op])
            total = term if total is None else total + term
        for f in range(faces):
            here = d_refs[l][f] + total[:, f * blk : f * blk + blk]
            applied = off_layer(here, d_refs[1 - l][f], ch_ref, cl_ref, l, f, group)
            pre_refs[l][f] = r_refs[l][f] - applied
            if with_x:
                x_outs[l][f] = x_refs[l][f] + d_refs[l][f]


def finish_kernel(group, coef, layer, halo_ref, pre_ref, hh_ref, hl_ref, *rest):
    for f in range(halo_ref.shape[0]):
        residual = pre_ref[f] - off_layer(0.0, halo_ref[f], hh_ref, hl_ref, layer, f, group)
        if coef is None:
            rest[0][f] = residual
        else:
            d_ref, r_out, d_out = rest
            r_out[f] = residual
            d_out[f] = coef[0] * d_ref[f] + coef[1] * residual


def last_kernel(
    group, halo_ref, pre_ref, r0_ref, x0_ref, x1_ref, hh_ref, hl_ref, send_ref, buffer, sems
):
    copies = []

    def send(k, l, value):
        for f in range(halo_ref.shape[0]):
            buffer[:, k, l, f] = value(f).reshape(-1, group, value(f).shape[-1])
        copies.append(
            pltpu.make_async_copy(buffer.at[:, k, l], send_ref.at[:, k, l], sems.at[k, l])
        )
        copies[-1].start()

    send(0, 0, lambda f: x0_ref[f])
    send(0, 1, lambda f: x1_ref[f])
    send(1, 0, lambda f: r0_ref[f])
    ends = [
        pre_ref[f] - off_layer(0.0, halo_ref[f], hh_ref, hl_ref, 1, f, group)
        for f in range(halo_ref.shape[0])
    ]
    send(1, 1, lambda f: ends[f])
    for copy in copies:
        copy.wait()


MIB = 1 << 20


def call(
    body, outs, args, flops=0, limit=6, in_space=pltpu.VMEM, out_space=pltpu.VMEM, scratch=()
):
    size = sum(a.size * a.dtype.itemsize for a in args) + sum(
        o.size * o.dtype.itemsize for o in outs
    )
    return pl.pallas_call(
        body,
        out_shape=outs,
        in_specs=[pl.BlockSpec(memory_space=in_space) for _ in args],
        out_specs=[pl.BlockSpec(memory_space=out_space) for _ in outs],
        scratch_shapes=list(scratch),
        compiler_params=pltpu.CompilerParams(vmem_limit_bytes=limit * MIB),
        cost_estimate=pl.CostEstimate(flops=flops, bytes_accessed=size, transcendentals=0),
    )(*args)


def shape(dims, dtype=F32):
    return jax.ShapeDtypeStruct(tuple(dims), dtype)


def prepare(mean_operator, field_operators, adjacency, mode_masks, modes_dev, bits):
    layers, faces, blk, wide = mean_operator.shape
    ops = bits + 1
    full = faces * blk

    def layer_of(spot):
        lead = place()[1]
        return jnp.where(spot == 0, lead, 1 - lead)

    dense_spec = pl.BlockSpec((1, 1, full, full), lambda l, op, *_: (l, op, 0, 0))
    side_spec = pl.BlockSpec((1, 1, faces, blk, blk), lambda l, op, *_: (l, op, 0, 0, 0))
    grid_spec = pltpu.PrefetchScalarGridSpec(
        num_scalar_prefetch=2,
        grid=(layers, ops),
        in_specs=[
            pl.BlockSpec(
                (1, faces, blk, wide), lambda l, op, masks, adj: (layer_of(l), 0, 0, 0)
            ),
            pl.BlockSpec(
                (1, 1, faces, blk, wide),
                lambda l, op, masks, adj: (field_of(masks, op, modes_dev), layer_of(l), 0, 0, 0),
            ),
        ],
        out_specs=[dense_spec] * 2 + [side_spec] * 4,
        scratch_shapes=[pltpu.VMEM((faces, full, blk), F32)],
    )
    dense = shape((layers, ops, full, full), BF16)
    side = shape((layers, ops, faces, blk, blk), BF16)
    return pl.pallas_call(
        prepare_kernel,
        grid_spec=grid_spec,
        out_shape=[dense] * 2 + [side] * 4,
        compiler_params=pltpu.CompilerParams(vmem_limit_bytes=56 * MIB),
        cost_estimate=pl.CostEstimate(flops=10**8, bytes_accessed=36 * MIB, transcendentals=0),
    )(mode_masks, adjacency, mean_operator, field_operators)


def pair_list(count, modes, inner):
    half = modes // 2
    pairs = []
    for s in range(count):
        t = (s + 1 if (s % 2 == 0) == inner else s - 1) % count
        turn = half if (s // 2 - t // 2) % 2 else 0
        pairs += [(s * modes + m, t * modes + (m ^ turn)) for m in range(modes)]
    return pairs


def per_device(source_field, mean_operator, field_operators, adjacency, mode_masks):
    layers, faces, blk, modes_dev = source_field.shape
    count, modes = lax.axis_size("space"), lax.axis_size("mode")
    bits = modes.bit_length() - 1
    group = modes_dev // modes
    rows = modes * group
    pieces = shape((modes, layers, faces, group, blk))
    layer = shape((faces, rows, blk))

    (sent,) = call(
        split_kernel,
        [pieces],
        [source_field],
        limit=60,
        in_space=pltpu.HBM,
        out_space=pltpu.HBM,
        scratch=[
            pltpu.VMEM(source_field.shape, F32),
            pltpu.VMEM(pieces.shape, F32),
            pltpu.SemaphoreType.DMA((layers, faces)),
            pltpu.SemaphoreType.DMA((layers,)),
        ],
    )
    got = lax.all_to_all(sent, "mode", 0, 0, tiled=True)
    weights = prepare(
        mean_operator, field_operators, adjacency, mode_masks, modes_dev, bits
    )
    got, *weights = lax.optimization_barrier((got, *weights))
    dh, dl, hh, hl, ch, cl = weights
    b = [got[:, l].transpose(1, 0, 2, 3).reshape(faces, rows, blk) for l in range(layers)]

    links = [pair_list(count, modes, True), pair_list(count, modes, False)]
    sigma = THETA / DELTA
    rho = 1.0 / sigma
    d, r = [v / THETA for v in b], b
    flops = 2 * rows * blk * blk * 3 * (bits + 1) * faces
    for step in range(DEGREE):
        last = step == DEGREE - 1
        halo = [lax.ppermute(d[l], AXES, links[l]) for l in range(layers)]
        pre0, pre1, *x_next = call(
            functools.partial(local_kernel, group, step > 0),
            [layer] * (4 if step else 2),
            [*d, *r, *(x if step else []), dh, dl, ch, cl],
        )
        pre = [pre0, pre1]
        x = x_next if step else d
        rho_new = 1.0 / (2.0 * sigma - rho)
        coef = (rho_new * rho, 2.0 * rho_new / DELTA)
        rho = rho_new
        if not last:
            fresh = []
            for l in range(layers):
                if fresh:
                    pre[l], _ = lax.optimization_barrier((pre[l], fresh[0][1]))
                fresh.append(
                    call(
                        functools.partial(finish_kernel, group, coef, l),
                        [layer, layer],
                        [halo[l], pre[l], hh, hl, d[l]],
                    )
                )
            r, d = zip(*fresh)
    (r_end,) = call(
        functools.partial(finish_kernel, group, None, 0), [layer], [halo[0], pre[0], hh, hl]
    )
    both = (modes, 2) + pieces.shape[1:]
    (send,) = call(
        functools.partial(last_kernel, group),
        [shape(both)],
        [halo[1], pre[1], r_end, *x, hh, hl],
        limit=12,
        out_space=pltpu.HBM,
        scratch=[pltpu.VMEM(both, F32), pltpu.SemaphoreType.DMA((2, layers))],
    )
    back = lax.all_to_all(send, "mode", 0, 0, tiled=True)
    field = shape(source_field.shape)
    return tuple(
        call(
            join_kernel,
            [field, field],
            [back],
            limit=12,
            out_space=pltpu.HBM,
            scratch=[
                pltpu.VMEM((2,) + source_field.shape, F32),
                pltpu.SemaphoreType.DMA((2, layers)),
            ],
        )
    )


def solution(mesh):
    in_specs = (
        P("space", None, None, "mode"),
        P("space", None, None, None),
        P(None, "space", None, None, None),
        P("space", None, None),
        P(),
    )
    out_specs = (P("space", None, None, "mode"), P("space", None, None, "mode"))
    return jax.shard_map(
        per_device, mesh=mesh, in_specs=in_specs, out_specs=out_specs, check_vma=False
    )
```

```python
import functools

import jax
import jax.numpy as jnp
from jax import lax
from jax.experimental import pallas as pl
from jax.experimental.pallas import tpu as pltpu
from jax.sharding import PartitionSpec as P

DEGREE = 4
COUPLING = 0.5773502691896258
THETA = 1.0
DELTA = 0.7
AXES = ("space", "mode")
F32 = jnp.float32
BF16 = jnp.bfloat16
NT = (((1,), (1,)), ((), ()))


def split2(value):
    high = value.astype(BF16)
    return high, (value - high.astype(F32)).astype(BF16)


def dot_nt(left, right):
    return lax.dot_general(left, right, NT, preferred_element_type=F32)


def swap_rows(value, bit, group):
    step = group << bit
    count = value.shape[0] // step
    return jnp.concatenate(
        [value[(i ^ 1) * step : (i ^ 1) * step + step] for i in range(count)], axis=0
    )


def permuted(value, op, group):
    return value if op == 0 else swap_rows(value, op - 1, group)


def place():
    slab = lax.axis_index("space").astype(jnp.int32)
    return lax.shift_right_logical(slab, 1) & 1, 1 - (slab & 1)


def split_kernel(field_ref, out_ref, arrived, laid, in_sems, out_sems):
    pieces, layers, faces, group, blk = out_ref.shape
    half = pieces // 2
    flip, lead = place()
    first = flip * half
    second = half - first
    ins, outs = [], []
    for l in range(layers):
        at = lead if l == 0 else 1 - lead
        for f in range(faces):
            ins.append(
                pltpu.make_async_copy(field_ref.at[at, f], arrived.at[l, f], in_sems.at[l, f])
            )
            ins[-1].start()
    for l in range(layers):
        for f in range(faces):
            ins[l * faces + f].wait()
            for at, start in enumerate((first, second)):
                columns = arrived[l, f, :, at * half * group : (at + 1) * half * group]
                laid[pl.ds(start, half), l, f] = columns.T.reshape(half, group, blk)
        outs.append(pltpu.make_async_copy(laid.at[:, l], out_ref.at[:, l], out_sems.at[l]))
        outs[-1].start()
    for copy in outs:
        copy.wait()


def join_kernel(in_ref, x_ref, r_ref, buffer, sems):
    pieces, fields, layers, faces, group, blk = in_ref.shape
    half = pieces // 2
    flip, lead = place()
    first = flip * half
    second = half - first
    copies = []
    for k, out_ref in enumerate((x_ref, r_ref)):
        for l in range(layers):
            at = lead if l == 0 else 1 - lead
            for f in range(faces):
                low = in_ref[pl.ds(first, half), k, l, f].reshape(half * group, blk)
                top = in_ref[pl.ds(second, half), k, l, f].reshape(half * group, blk)
                buffer[k, l, f] = jnp.concatenate([low.T, top.T], axis=1)
            copies.append(pltpu.make_async_copy(buffer.at[k, l], out_ref.at[at], sems.at[k, l]))
            copies[-1].start()
    for copy in copies:
        copy.wait()


def field_of(masks, op, modes_dev):
    want = modes_dev * lax.shift_left(jnp.int32(1), jnp.maximum(op - 1, 0))
    found = jnp.int32(0)
    for j in range(masks.shape[0]):
        found = found + jnp.where(masks[j] == want, j, 0)
    return found


def prepare_kernel(
    masks_ref, adj_ref, mean_ref, field_ref,
    dh_ref, dl_ref, hh_ref, hl_ref, ch_ref, cl_ref, dense,
):
    spot = pl.program_id(0)
    op = pl.program_id(1)
    faces, blk = mean_ref.shape[1], mean_ref.shape[2]
    lead = place()[1]
    layer = jnp.where(spot == 0, lead, 1 - lead)
    halo_at = pl.multiple_of((1 + layer) * blk, blk)
    cross_at = pl.multiple_of((2 - layer) * blk, blk)
    slab = lax.axis_index("space").astype(jnp.int32)
    ends = (slab == 0) | (slab == lax.axis_size("space") - 1)
    inside = jnp.where((spot == 1) & ends, 0.0, 1.0).astype(F32)

    def build(src, scale):
        dense[...] = jnp.zeros_like(dense)
        for f in range(faces):
            rows = slice(f * blk, f * blk + blk)
            dense[f, rows] = src(f, 0)
            for s in range(4):
                other = adj_ref[layer, f, s]
                dense[other, rows] = dense[other, rows] + src(f, (3 + s) * blk)
        for g in range(faces):
            high, low = split2(dense[g] * scale)
            dh_ref[0, 0, :, g * blk : g * blk + blk] = high
            dl_ref[0, 0, :, g * blk : g * blk + blk] = low
        for f in range(faces):
            hh_ref[0, 0, f], hl_ref[0, 0, f] = split2(src(f, halo_at) * scale * inside)
            ch_ref[0, 0, f], cl_ref[0, 0, f] = split2(src(f, cross_at) * scale)

    @pl.when(op == 0)
    def _():
        build(lambda f, k: mean_ref[0, f, :, pl.ds(k, blk)], 1.0)

    @pl.when(op > 0)
    def _():
        build(lambda f, k: field_ref[0, 0, f, :, pl.ds(k, blk)], COUPLING)


def off_layer(total, field, op_h, op_l, layer, f, group):
    high, low = split2(field)
    ops = range(op_h.shape[1])
    heavy = [op_h[layer, op, f] for op in ops]
    wide = [jnp.concatenate([op_h[layer, op, f], op_l[layer, op, f]], axis=0) for op in ops]
    tops = jnp.concatenate([permuted(high, op, group) for op in ops], axis=1)
    rest = jnp.concatenate([permuted(low, op, group) for op in ops], axis=1)
    both = dot_nt(tops, jnp.concatenate(wide, axis=1))
    blk = field.shape[1]
    small = both[:, blk:] + dot_nt(rest, jnp.concatenate(heavy, axis=1))
    return total + (both[:, :blk] + small)


def local_kernel(group, with_x, *refs):
    count = 6 if with_x else 4
    d_refs, r_refs, x_refs = refs[0:2], refs[2:4], refs[4:count]
    dh_ref, dl_ref, ch_ref, cl_ref = refs[count : count + 4]
    pre_refs = refs[count + 4 : count + 6]
    x_outs = refs[count + 6 :]
    faces, rows, blk = d_refs[0].shape
    ops = dh_ref.shape[1]
    for l in range(2):
        parts = [split2(d_refs[l][f]) for f in range(faces)]
        high = jnp.concatenate([p[0] for p in parts], axis=1)
        low = jnp.concatenate([p[1] for p in parts], axis=1)
        total = None
        for op in range(ops):
            ph, plow = permuted(high, op, group), permuted(low, op, group)
            term = dot_nt(ph, dh_ref[l, op]) + dot_nt(plow, dh_ref[l, op]) + dot_nt(ph, dl_ref[l, op])
            total = term if total is None else total + term
        for f in range(faces):
            here = d_refs[l][f] + total[:, f * blk : f * blk + blk]
            applied = off_layer(here, d_refs[1 - l][f], ch_ref, cl_ref, l, f, group)
            pre_refs[l][f] = r_refs[l][f] - applied
            if with_x:
                x_outs[l][f] = x_refs[l][f] + d_refs[l][f]


def finish_kernel(group, coef, layer, halo_ref, pre_ref, hh_ref, hl_ref, *rest):
    for f in range(halo_ref.shape[0]):
        residual = pre_ref[f] - off_layer(0.0, halo_ref[f], hh_ref, hl_ref, layer, f, group)
        if coef is None:
            rest[0][f] = residual
        else:
            d_ref, r_out, d_out = rest
            r_out[f] = residual
            d_out[f] = coef[0] * d_ref[f] + coef[1] * residual


def last_kernel(
    group, halo_ref, pre_ref, r0_ref, x0_ref, x1_ref, hh_ref, hl_ref, send_ref, buffer, sems
):
    copies = []

    def send(k, l, value):
        for f in range(halo_ref.shape[0]):
            buffer[:, k, l, f] = value(f).reshape(-1, group, value(f).shape[-1])
        copies.append(
            pltpu.make_async_copy(buffer.at[:, k, l], send_ref.at[:, k, l], sems.at[k, l])
        )
        copies[-1].start()

    send(0, 0, lambda f: x0_ref[f])
    send(0, 1, lambda f: x1_ref[f])
    send(1, 0, lambda f: r0_ref[f])
    ends = [
        pre_ref[f] - off_layer(0.0, halo_ref[f], hh_ref, hl_ref, 1, f, group)
        for f in range(halo_ref.shape[0])
    ]
    send(1, 1, lambda f: ends[f])
    for copy in copies:
        copy.wait()


MIB = 1 << 20


def call(
    body, outs, args, flops=0, limit=6, in_space=pltpu.VMEM, out_space=pltpu.VMEM, scratch=()
):
    size = sum(a.size * a.dtype.itemsize for a in args) + sum(
        o.size * o.dtype.itemsize for o in outs
    )
    return pl.pallas_call(
        body,
        out_shape=outs,
        in_specs=[pl.BlockSpec(memory_space=in_space) for _ in args],
        out_specs=[pl.BlockSpec(memory_space=out_space) for _ in outs],
        scratch_shapes=list(scratch),
        compiler_params=pltpu.CompilerParams(vmem_limit_bytes=limit * MIB),
        cost_estimate=pl.CostEstimate(flops=flops, bytes_accessed=size, transcendentals=0),
    )(*args)


def shape(dims, dtype=F32):
    return jax.ShapeDtypeStruct(tuple(dims), dtype)


def prepare(mean_operator, field_operators, adjacency, mode_masks, modes_dev, bits):
    layers, faces, blk, wide = mean_operator.shape
    ops = bits + 1
    full = faces * blk

    def layer_of(spot):
        lead = place()[1]
        return jnp.where(spot == 0, lead, 1 - lead)

    dense_spec = pl.BlockSpec((1, 1, full, full), lambda l, op, *_: (l, op, 0, 0))
    side_spec = pl.BlockSpec((1, 1, faces, blk, blk), lambda l, op, *_: (l, op, 0, 0, 0))
    grid_spec = pltpu.PrefetchScalarGridSpec(
        num_scalar_prefetch=2,
        grid=(layers, ops),
        in_specs=[
            pl.BlockSpec(
                (1, faces, blk, wide), lambda l, op, masks, adj: (layer_of(l), 0, 0, 0)
            ),
            pl.BlockSpec(
                (1, 1, faces, blk, wide),
                lambda l, op, masks, adj: (field_of(masks, op, modes_dev), layer_of(l), 0, 0, 0),
            ),
        ],
        out_specs=[dense_spec] * 2 + [side_spec] * 4,
        scratch_shapes=[pltpu.VMEM((faces, full, blk), F32)],
    )
    dense = shape((layers, ops, full, full), BF16)
    side = shape((layers, ops, faces, blk, blk), BF16)
    return pl.pallas_call(
        prepare_kernel,
        grid_spec=grid_spec,
        out_shape=[dense] * 2 + [side] * 4,
        compiler_params=pltpu.CompilerParams(vmem_limit_bytes=56 * MIB),
        cost_estimate=pl.CostEstimate(flops=10**8, bytes_accessed=36 * MIB, transcendentals=0),
    )(mode_masks, adjacency, mean_operator, field_operators)


def pair_list(count, modes, inner):
    half = modes // 2
    pairs = []
    for s in range(count):
        t = (s + 1 if (s % 2 == 0) == inner else s - 1) % count
        turn = half if (s // 2 - t // 2) % 2 else 0
        pairs += [(s * modes + m, t * modes + (m ^ turn)) for m in range(modes)]
    return pairs


def per_device(source_field, mean_operator, field_operators, adjacency, mode_masks):
    layers, faces, blk, modes_dev = source_field.shape
    count, modes = lax.axis_size("space"), lax.axis_size("mode")
    bits = modes.bit_length() - 1
    group = modes_dev // modes
    rows = modes * group
    pieces = shape((modes, layers, faces, group, blk))
    layer = shape((faces, rows, blk))

    (sent,) = call(
        split_kernel,
        [pieces],
        [source_field],
        limit=60,
        in_space=pltpu.HBM,
        out_space=pltpu.HBM,
        scratch=[
            pltpu.VMEM(source_field.shape, F32),
            pltpu.VMEM(pieces.shape, F32),
            pltpu.SemaphoreType.DMA((layers, faces)),
            pltpu.SemaphoreType.DMA((layers,)),
        ],
    )
    got = lax.all_to_all(sent, "mode", 0, 0, tiled=True)
    weights = prepare(
        mean_operator, field_operators, adjacency, mode_masks, modes_dev, bits
    )
    got, *weights = lax.optimization_barrier((got, *weights))
    dh, dl, hh, hl, ch, cl = weights
    b = [got[:, l].transpose(1, 0, 2, 3).reshape(faces, rows, blk) for l in range(layers)]

    links = [pair_list(count, modes, True), pair_list(count, modes, False)]
    sigma = THETA / DELTA
    rho = 1.0 / sigma
    d, r = [v / THETA for v in b], b
    flops = 2 * rows * blk * blk * 3 * (bits + 1) * faces
    for step in range(DEGREE):
        last = step == DEGREE - 1
        halo = [lax.ppermute(d[l], AXES, links[l]) for l in range(layers)]
        pre0, pre1, *x_next = call(
            functools.partial(local_kernel, group, step > 0),
            [layer] * (4 if step else 2),
            [*d, *r, *(x if step else []), dh, dl, ch, cl],
        )
        pre = [pre0, pre1]
        x = x_next if step else d
        rho_new = 1.0 / (2.0 * sigma - rho)
        coef = (rho_new * rho, 2.0 * rho_new / DELTA)
        rho = rho_new
        if not last:
            fresh = []
            for l in range(layers):
                if fresh:
                    pre[l], _ = lax.optimization_barrier((pre[l], fresh[0][1]))
                fresh.append(
                    call(
                        functools.partial(finish_kernel, group, coef, l),
                        [layer, layer],
                        [halo[l], pre[l], hh, hl, d[l]],
                    )
                )
            r, d = zip(*fresh)
    (r_end,) = call(
        functools.partial(finish_kernel, group, None, 0), [layer], [halo[0], pre[0], hh, hl]
    )
    both = (modes, 2) + pieces.shape[1:]
    (send,) = call(
        functools.partial(last_kernel, group),
        [shape(both)],
        [halo[1], pre[1], r_end, *x, hh, hl],
        limit=12,
        out_space=pltpu.HBM,
        scratch=[pltpu.VMEM(both, F32), pltpu.SemaphoreType.DMA((2, layers))],
    )
    back = lax.all_to_all(send, "mode", 0, 0, tiled=True)
    field = shape(source_field.shape)
    return tuple(
        call(
            join_kernel,
            [field, field],
            [back],
            limit=12,
            out_space=pltpu.HBM,
            scratch=[
                pltpu.VMEM((2,) + source_field.shape, F32),
                pltpu.SemaphoreType.DMA((2, layers)),
            ],
        )
    )


def solution(mesh):
    in_specs = (
        P("space", None, None, "mode"),
        P("space", None, None, None),
        P(None, "space", None, None, None),
        P("space", None, None),
        P(),
    )
    out_specs = (P("space", None, None, "mode"), P("space", None, None, "mode"))
    return jax.shard_map(
        per_device, mesh=mesh, in_specs=in_specs, out_specs=out_specs, check_vma=False
    )
```

```python
import functools

import jax
import jax.numpy as jnp
from jax import lax
from jax.experimental import pallas as pl
from jax.experimental.pallas import tpu as pltpu
from jax.sharding import PartitionSpec as P

DEGREE = 4
COUPLING = 0.5773502691896258
THETA = 1.0
DELTA = 0.7
AXES = ("space", "mode")
F32 = jnp.float32
BF16 = jnp.bfloat16
NT = (((1,), (1,)), ((), ()))


def split2(value):
    high = value.astype(BF16)
    return high, (value - high.astype(F32)).astype(BF16)


def dot_nt(left, right):
    return lax.dot_general(left, right, NT, preferred_element_type=F32)


def swap_rows(value, bit, group):
    step = group << bit
    count = value.shape[0] // step
    return jnp.concatenate(
        [value[(i ^ 1) * step : (i ^ 1) * step + step] for i in range(count)], axis=0
    )


def permuted(value, op, group):
    return value if op == 0 else swap_rows(value, op - 1, group)


def place():
    slab = lax.axis_index("space").astype(jnp.int32)
    return lax.shift_right_logical(slab + 1, 1) & 1, 1 - (slab & 1)


def split_kernel(field_ref, out_ref, arrived, laid, in_sems, out_sems):
    pieces, layers, faces, group, blk = out_ref.shape
    half = pieces // 2
    flip, lead = place()
    first = flip * half
    second = half - first
    ins, outs = [], []
    for l in range(layers):
        at = lead if l == 0 else 1 - lead
        for f in range(faces):
            ins.append(
                pltpu.make_async_copy(field_ref.at[at, f], arrived.at[l, f], in_sems.at[l, f])
            )
            ins[-1].start()
    for l in range(layers):
        for f in range(faces):
            ins[l * faces + f].wait()
            rows = arrived[l, f].T.reshape(pieces, group, blk)
            laid[pl.ds(first, half), l, f] = rows[:half]
            laid[pl.ds(second, half), l, f] = rows[half:]
        outs.append(pltpu.make_async_copy(laid.at[:, l], out_ref.at[:, l], out_sems.at[l]))
        outs[-1].start()
    for copy in outs:
        copy.wait()


def join_kernel(in_ref, x_ref, r_ref, buffer, sems):
    pieces, fields, layers, faces, group, blk = in_ref.shape
    half = pieces // 2
    flip, lead = place()
    first = flip * half
    second = half - first
    copies = []
    for k, out_ref in enumerate((x_ref, r_ref)):
        for l in range(layers):
            at = lead if l == 0 else 1 - lead
            for f in range(faces):
                low = in_ref[pl.ds(first, half), k, l, f].reshape(half * group, blk)
                top = in_ref[pl.ds(second, half), k, l, f].reshape(half * group, blk)
                buffer[k, l, f] = jnp.concatenate([low.T, top.T], axis=1)
            copies.append(pltpu.make_async_copy(buffer.at[k, l], out_ref.at[at], sems.at[k, l]))
            copies[-1].start()
    for copy in copies:
        copy.wait()


def field_of(masks, op, modes_dev):
    want = modes_dev * lax.shift_left(jnp.int32(1), jnp.maximum(op - 1, 0))
    found = jnp.int32(0)
    for j in range(masks.shape[0]):
        found = found + jnp.where(masks[j] == want, j, 0)
    return found


def prepare_kernel(
    masks_ref, adj_ref, mean_ref, field_ref,
    dh_ref, dl_ref, hh_ref, hl_ref, ch_ref, cl_ref, dense,
):
    spot = pl.program_id(0)
    op = pl.program_id(1)
    faces, blk = mean_ref.shape[1], mean_ref.shape[2]
    lead = place()[1]
    layer = jnp.where(spot == 0, lead, 1 - lead)
    halo_at = pl.multiple_of((1 + layer) * blk, blk)
    cross_at = pl.multiple_of((2 - layer) * blk, blk)
    slab = lax.axis_index("space").astype(jnp.int32)
    ends = (slab == 0) | (slab == lax.axis_size("space") - 1)
    inside = jnp.where((spot == 1) & ends, 0.0, 1.0).astype(F32)

    def build(src, scale):
        dense[...] = jnp.zeros_like(dense)
        for f in range(faces):
            rows = slice(f * blk, f * blk + blk)
            dense[f, rows] = src(f, 0)
            for s in range(4):
                other = adj_ref[layer, f, s]
                dense[other, rows] = dense[other, rows] + src(f, (3 + s) * blk)
        for g in range(faces):
            high, low = split2(dense[g] * scale)
            dh_ref[0, 0, :, g * blk : g * blk + blk] = high
            dl_ref[0, 0, :, g * blk : g * blk + blk] = low
        for f in range(faces):
            hh_ref[0, 0, f], hl_ref[0, 0, f] = split2(src(f, halo_at) * scale * inside)
            ch_ref[0, 0, f], cl_ref[0, 0, f] = split2(src(f, cross_at) * scale)

    @pl.when(op == 0)
    def _():
        build(lambda f, k: mean_ref[0, f, :, pl.ds(k, blk)], 1.0)

    @pl.when(op > 0)
    def _():
        build(lambda f, k: field_ref[0, 0, f, :, pl.ds(k, blk)], COUPLING)


def off_layer(total, field, op_h, op_l, layer, f, group):
    high, low = split2(field)
    ops = range(op_h.shape[1])
    heavy = [op_h[layer, op, f] for op in ops]
    wide = [jnp.concatenate([op_h[layer, op, f], op_l[layer, op, f]], axis=0) for op in ops]
    tops = jnp.concatenate([permuted(high, op, group) for op in ops], axis=1)
    rest = jnp.concatenate([permuted(low, op, group) for op in ops], axis=1)
    both = dot_nt(tops, jnp.concatenate(wide, axis=1))
    blk = field.shape[1]
    small = both[:, blk:] + dot_nt(rest, jnp.concatenate(heavy, axis=1))
    return total + (both[:, :blk] + small)


def local_kernel(group, with_x, *refs):
    count = 6 if with_x else 4
    d_refs, r_refs, x_refs = refs[0:2], refs[2:4], refs[4:count]
    dh_ref, dl_ref, ch_ref, cl_ref = refs[count : count + 4]
    pre_refs = refs[count + 4 : count + 6]
    x_outs = refs[count + 6 :]
    faces, rows, blk = d_refs[0].shape
    ops = dh_ref.shape[1]
    for l in range(2):
        parts = [split2(d_refs[l][f]) for f in range(faces)]
        high = jnp.concatenate([p[0] for p in parts], axis=1)
        low = jnp.concatenate([p[1] for p in parts], axis=1)
        total = None
        for op in range(ops):
            ph, plow = permuted(high, op, group), permuted(low, op, group)
            term = dot_nt(ph, dh_ref[l, op]) + dot_nt(plow, dh_ref[l, op]) + dot_nt(ph, dl_ref[l, op])
            total = term if total is None else total + term
        for f in range(faces):
            here = d_refs[l][f] + total[:, f * blk : f * blk + blk]
            applied = off_layer(here, d_refs[1 - l][f], ch_ref, cl_ref, l, f, group)
            pre_refs[l][f] = r_refs[l][f] - applied
            if with_x:
                x_outs[l][f] = x_refs[l][f] + d_refs[l][f]


def finish_kernel(group, coef, layer, halo_ref, pre_ref, hh_ref, hl_ref, *rest):
    for f in range(halo_ref.shape[0]):
        residual = pre_ref[f] - off_layer(0.0, halo_ref[f], hh_ref, hl_ref, layer, f, group)
        if coef is None:
            rest[0][f] = residual
        else:
            d_ref, r_out, d_out = rest
            r_out[f] = residual
            d_out[f] = coef[0] * d_ref[f] + coef[1] * residual


def last_kernel(
    group, halo_ref, pre_ref, r0_ref, x0_ref, x1_ref, hh_ref, hl_ref, send_ref, buffer, sems
):
    copies = []

    def send(k, l, value):
        for f in range(halo_ref.shape[0]):
            buffer[:, k, l, f] = value(f).reshape(-1, group, value(f).shape[-1])
        copies.append(
            pltpu.make_async_copy(buffer.at[:, k, l], send_ref.at[:, k, l], sems.at[k, l])
        )
        copies[-1].start()

    send(0, 0, lambda f: x0_ref[f])
    send(0, 1, lambda f: x1_ref[f])
    send(1, 0, lambda f: r0_ref[f])
    ends = [
        pre_ref[f] - off_layer(0.0, halo_ref[f], hh_ref, hl_ref, 1, f, group)
        for f in range(halo_ref.shape[0])
    ]
    send(1, 1, lambda f: ends[f])
    for copy in copies:
        copy.wait()


MIB = 1 << 20


def call(
    body, outs, args, flops=0, limit=6, in_space=pltpu.VMEM, out_space=pltpu.VMEM, scratch=()
):
    size = sum(a.size * a.dtype.itemsize for a in args) + sum(
        o.size * o.dtype.itemsize for o in outs
    )
    return pl.pallas_call(
        body,
        out_shape=outs,
        in_specs=[pl.BlockSpec(memory_space=in_space) for _ in args],
        out_specs=[pl.BlockSpec(memory_space=out_space) for _ in outs],
        scratch_shapes=list(scratch),
        compiler_params=pltpu.CompilerParams(vmem_limit_bytes=limit * MIB),
        cost_estimate=pl.CostEstimate(flops=flops, bytes_accessed=size, transcendentals=0),
    )(*args)


def shape(dims, dtype=F32):
    return jax.ShapeDtypeStruct(tuple(dims), dtype)


def prepare(mean_operator, field_operators, adjacency, mode_masks, modes_dev, bits):
    layers, faces, blk, wide = mean_operator.shape
    ops = bits + 1
    full = faces * blk

    def layer_of(spot):
        lead = place()[1]
        return jnp.where(spot == 0, lead, 1 - lead)

    dense_spec = pl.BlockSpec((1, 1, full, full), lambda l, op, *_: (l, op, 0, 0))
    side_spec = pl.BlockSpec((1, 1, faces, blk, blk), lambda l, op, *_: (l, op, 0, 0, 0))
    grid_spec = pltpu.PrefetchScalarGridSpec(
        num_scalar_prefetch=2,
        grid=(layers, ops),
        in_specs=[
            pl.BlockSpec(
                (1, faces, blk, wide), lambda l, op, masks, adj: (layer_of(l), 0, 0, 0)
            ),
            pl.BlockSpec(
                (1, 1, faces, blk, wide),
                lambda l, op, masks, adj: (field_of(masks, op, modes_dev), layer_of(l), 0, 0, 0),
            ),
        ],
        out_specs=[dense_spec] * 2 + [side_spec] * 4,
        scratch_shapes=[pltpu.VMEM((faces, full, blk), F32)],
    )
    dense = shape((layers, ops, full, full), BF16)
    side = shape((layers, ops, faces, blk, blk), BF16)
    return pl.pallas_call(
        prepare_kernel,
        grid_spec=grid_spec,
        out_shape=[dense] * 2 + [side] * 4,
        compiler_params=pltpu.CompilerParams(vmem_limit_bytes=56 * MIB),
        cost_estimate=pl.CostEstimate(flops=10**8, bytes_accessed=36 * MIB, transcendentals=0),
    )(mode_masks, adjacency, mean_operator, field_operators)


def pair_list(count, modes, inner):
    half = modes // 2
    pairs = []
    for s in range(count):
        t = (s + 1 if (s % 2 == 0) == inner else s - 1) % count
        turn = half if ((s + 1) // 2 - (t + 1) // 2) % 2 else 0
        pairs += [(s * modes + m, t * modes + (m ^ turn)) for m in range(modes)]
    return pairs


def per_device(source_field, mean_operator, field_operators, adjacency, mode_masks):
    layers, faces, blk, modes_dev = source_field.shape
    count, modes = lax.axis_size("space"), lax.axis_size("mode")
    bits = modes.bit_length() - 1
    group = modes_dev // modes
    rows = modes * group
    pieces = shape((modes, layers, faces, group, blk))
    layer = shape((faces, rows, blk))

    (sent,) = call(
        split_kernel,
        [pieces],
        [source_field],
        limit=60,
        in_space=pltpu.HBM,
        out_space=pltpu.HBM,
        scratch=[
            pltpu.VMEM(source_field.shape, F32),
            pltpu.VMEM(pieces.shape, F32),
            pltpu.SemaphoreType.DMA((layers, faces)),
            pltpu.SemaphoreType.DMA((layers,)),
        ],
    )
    got = lax.all_to_all(sent, "mode", 0, 0, tiled=True)
    weights = prepare(
        mean_operator, field_operators, adjacency, mode_masks, modes_dev, bits
    )
    got, *weights = lax.optimization_barrier((got, *weights))
    dh, dl, hh, hl, ch, cl = weights
    b = [got[:, l].transpose(1, 0, 2, 3).reshape(faces, rows, blk) for l in range(layers)]

    links = [pair_list(count, modes, True), pair_list(count, modes, False)]
    sigma = THETA / DELTA
    rho = 1.0 / sigma
    d, r = [v / THETA for v in b], b
    flops = 2 * rows * blk * blk * 3 * (bits + 1) * faces
    for step in range(DEGREE):
        last = step == DEGREE - 1
        halo = [lax.ppermute(d[l], AXES, links[l]) for l in range(layers)]
        pre0, pre1, *x_next = call(
            functools.partial(local_kernel, group, step > 0),
            [layer] * (4 if step else 2),
            [*d, *r, *(x if step else []), dh, dl, ch, cl],
        )
        pre = [pre0, pre1]
        x = x_next if step else d
        rho_new = 1.0 / (2.0 * sigma - rho)
        coef = (rho_new * rho, 2.0 * rho_new / DELTA)
        rho = rho_new
        if not last:
            fresh = []
            for l in range(layers):
                if fresh:
                    pre[l], _ = lax.optimization_barrier((pre[l], fresh[0][1]))
                fresh.append(
                    call(
                        functools.partial(finish_kernel, group, coef, l),
                        [layer, layer],
                        [halo[l], pre[l], hh, hl, d[l]],
                    )
                )
            r, d = zip(*fresh)
    (r_end,) = call(
        functools.partial(finish_kernel, group, None, 0), [layer], [halo[0], pre[0], hh, hl]
    )
    both = (modes, 2) + pieces.shape[1:]
    (send,) = call(
        functools.partial(last_kernel, group),
        [shape(both)],
        [halo[1], pre[1], r_end, *x, hh, hl],
        limit=12,
        out_space=pltpu.HBM,
        scratch=[pltpu.VMEM(both, F32), pltpu.SemaphoreType.DMA((2, layers))],
    )
    back = lax.all_to_all(send, "mode", 0, 0, tiled=True)
    field = shape(source_field.shape)
    return tuple(
        call(
            join_kernel,
            [field, field],
            [back],
            limit=12,
            out_space=pltpu.HBM,
            scratch=[
                pltpu.VMEM((2,) + source_field.shape, F32),
                pltpu.SemaphoreType.DMA((2, layers)),
            ],
        )
    )


def solution(mesh):
    in_specs = (
        P("space", None, None, "mode"),
        P("space", None, None, None),
        P(None, "space", None, None, None),
        P("space", None, None),
        P(),
    )
    out_specs = (P("space", None, None, "mode"), P("space", None, None, "mode"))
    return jax.shard_map(
        per_device, mesh=mesh, in_specs=in_specs, out_specs=out_specs, check_vma=False
    )
```

```python
import functools

import jax
import jax.numpy as jnp
from jax import lax
from jax.experimental import pallas as pl
from jax.experimental.pallas import tpu as pltpu
from jax.sharding import PartitionSpec as P

DEGREE = 4
COUPLING = 0.5773502691896258
THETA = 1.0
DELTA = 0.7
AXES = ("space", "mode")
F32 = jnp.float32
BF16 = jnp.bfloat16
NT = (((1,), (1,)), ((), ()))


def split2(value):
    high = value.astype(BF16)
    return high, (value - high.astype(F32)).astype(BF16)


def dot_nt(left, right):
    return lax.dot_general(left, right, NT, preferred_element_type=F32)


def swap_rows(value, bit, group):
    step = group << bit
    count = value.shape[0] // step
    return jnp.concatenate(
        [value[(i ^ 1) * step : (i ^ 1) * step + step] for i in range(count)], axis=0
    )


def permuted(value, op, group):
    return value if op == 0 else swap_rows(value, op - 1, group)


def place():
    slab = lax.axis_index("space").astype(jnp.int32)
    return lax.shift_right_logical(slab + 1, 1) & 1, 1 - (slab & 1)


def split_kernel(field_ref, out_ref, arrived, laid, in_sems, out_sems):
    pieces, layers, faces, group, blk = out_ref.shape
    half = pieces // 2
    flip, lead = place()
    first = flip * half
    second = half - first
    ins, outs = [], []
    for l in range(layers):
        at = lead if l == 0 else 1 - lead
        for f in range(faces):
            ins.append(
                pltpu.make_async_copy(field_ref.at[at, f], arrived.at[l, f], in_sems.at[l, f])
            )
            ins[-1].start()
    for l in range(layers):
        for f in range(faces):
            ins[l * faces + f].wait()
            rows = arrived[l, f].T.reshape(pieces, group, blk)
            laid[pl.ds(first, half), l, f] = rows[:half]
            laid[pl.ds(second, half), l, f] = rows[half:]
        outs.append(pltpu.make_async_copy(laid.at[:, l], out_ref.at[:, l], out_sems.at[l]))
        outs[-1].start()
    for copy in outs:
        copy.wait()


def join_kernel(in_ref, x_ref, r_ref, buffer, sems):
    pieces, fields, layers, faces, group, blk = in_ref.shape
    half = pieces // 2
    flip, lead = place()
    first = flip * half
    second = half - first
    copies = []
    for k, out_ref in enumerate((x_ref, r_ref)):
        for l in range(layers):
            at = lead if l == 0 else 1 - lead
            for f in range(faces):
                low = in_ref[pl.ds(first, half), k, l, f].reshape(half * group, blk)
                top = in_ref[pl.ds(second, half), k, l, f].reshape(half * group, blk)
                buffer[k, l, f] = jnp.concatenate([low.T, top.T], axis=1)
            copies.append(pltpu.make_async_copy(buffer.at[k, l], out_ref.at[at], sems.at[k, l]))
            copies[-1].start()
    for copy in copies:
        copy.wait()


def field_of(masks, op, modes_dev):
    want = modes_dev * lax.shift_left(jnp.int32(1), jnp.maximum(op - 1, 0))
    found = jnp.int32(0)
    for j in range(masks.shape[0]):
        found = found + jnp.where(masks[j] == want, j, 0)
    return found


def prepare_kernel(
    masks_ref, adj_ref, mean_ref, field_ref,
    dh_ref, dl_ref, hh_ref, hl_ref, ch_ref, cl_ref, dense,
):
    spot = pl.program_id(0)
    op = pl.program_id(1)
    faces, blk = mean_ref.shape[1], mean_ref.shape[2]
    lead = place()[1]
    layer = jnp.where(spot == 0, lead, 1 - lead)
    halo_at = pl.multiple_of((1 + layer) * blk, blk)
    cross_at = pl.multiple_of((2 - layer) * blk, blk)
    slab = lax.axis_index("space").astype(jnp.int32)
    ends = (slab == 0) | (slab == lax.axis_size("space") - 1)
    inside = jnp.where((spot == 1) & ends, 0.0, 1.0).astype(F32)

    def build(src, scale):
        dense[...] = jnp.zeros_like(dense)
        for f in range(faces):
            rows = slice(f * blk, f * blk + blk)
            dense[f, rows] = src(f, 0)
            for s in range(4):
                other = adj_ref[layer, f, s]
                dense[other, rows] = dense[other, rows] + src(f, (3 + s) * blk)
        for g in range(faces):
            high, low = split2(dense[g] * scale)
            dh_ref[0, 0, :, g * blk : g * blk + blk] = high
            dl_ref[0, 0, :, g * blk : g * blk + blk] = low
        for f in range(faces):
            hh_ref[0, 0, f], hl_ref[0, 0, f] = split2(src(f, halo_at) * scale * inside)
            ch_ref[0, 0, f], cl_ref[0, 0, f] = split2(src(f, cross_at) * scale)

    @pl.when(op == 0)
    def _():
        build(lambda f, k: mean_ref[0, f, :, pl.ds(k, blk)], 1.0)

    @pl.when(op > 0)
    def _():
        build(lambda f, k: field_ref[0, 0, f, :, pl.ds(k, blk)], COUPLING)


def off_layer(total, field, op_h, op_l, layer, f, group):
    high, low = split2(field)
    ops = range(op_h.shape[1])
    heavy = [op_h[layer, op, f] for op in ops]
    wide = [jnp.concatenate([op_h[layer, op, f], op_l[layer, op, f]], axis=0) for op in ops]
    tops = jnp.concatenate([permuted(high, op, group) for op in ops], axis=1)
    rest = jnp.concatenate([permuted(low, op, group) for op in ops], axis=1)
    both = dot_nt(tops, jnp.concatenate(wide, axis=1))
    blk = field.shape[1]
    small = both[:, blk:] + dot_nt(rest, jnp.concatenate(heavy, axis=1))
    return total + (both[:, :blk] + small)


def local_kernel(group, with_x, *refs):
    count = 6 if with_x else 4
    d_refs, r_refs, x_refs = refs[0:2], refs[2:4], refs[4:count]
    dh_ref, dl_ref, ch_ref, cl_ref = refs[count : count + 4]
    pre_refs = refs[count + 4 : count + 6]
    x_outs = refs[count + 6 :]
    faces, rows, blk = d_refs[0].shape
    ops = dh_ref.shape[1]
    for l in range(2):
        parts = [split2(d_refs[l][f]) for f in range(faces)]
        high = jnp.concatenate([p[0] for p in parts], axis=1)
        low = jnp.concatenate([p[1] for p in parts], axis=1)
        total = None
        for op in range(ops):
            ph, plow = permuted(high, op, group), permuted(low, op, group)
            term = dot_nt(ph, dh_ref[l, op]) + dot_nt(plow, dh_ref[l, op]) + dot_nt(ph, dl_ref[l, op])
            total = term if total is None else total + term
        for f in range(faces):
            here = d_refs[l][f] + total[:, f * blk : f * blk + blk]
            applied = off_layer(here, d_refs[1 - l][f], ch_ref, cl_ref, l, f, group)
            pre_refs[l][f] = r_refs[l][f] - applied
            if with_x:
                x_outs[l][f] = x_refs[l][f] + d_refs[l][f]


def finish_kernel(group, coef, layer, halo_ref, pre_ref, hh_ref, hl_ref, *rest):
    for f in range(halo_ref.shape[0]):
        residual = pre_ref[f] - off_layer(0.0, halo_ref[f], hh_ref, hl_ref, layer, f, group)
        if coef is None:
            rest[0][f] = residual
        else:
            d_ref, r_out, d_out = rest
            r_out[f] = residual
            d_out[f] = coef[0] * d_ref[f] + coef[1] * residual


def last_kernel(
    group, halo_ref, pre_ref, r0_ref, x0_ref, x1_ref, hh_ref, hl_ref, send_ref, buffer, sems
):
    copies = []

    def send(k, l, value):
        for f in range(halo_ref.shape[0]):
            buffer[:, k, l, f] = value(f).reshape(-1, group, value(f).shape[-1])
        copies.append(
            pltpu.make_async_copy(buffer.at[:, k, l], send_ref.at[:, k, l], sems.at[k, l])
        )
        copies[-1].start()

    send(0, 0, lambda f: x0_ref[f])
    send(0, 1, lambda f: x1_ref[f])
    send(1, 0, lambda f: r0_ref[f])
    ends = [
        pre_ref[f] - off_layer(0.0, halo_ref[f], hh_ref, hl_ref, 1, f, group)
        for f in range(halo_ref.shape[0])
    ]
    send(1, 1, lambda f: ends[f])
    for copy in copies:
        copy.wait()


MIB = 1 << 20


def call(
    body, outs, args, flops=0, limit=6, in_space=pltpu.VMEM, out_space=pltpu.VMEM, scratch=()
):
    size = sum(a.size * a.dtype.itemsize for a in args) + sum(
        o.size * o.dtype.itemsize for o in outs
    )
    return pl.pallas_call(
        body,
        out_shape=outs,
        in_specs=[pl.BlockSpec(memory_space=in_space) for _ in args],
        out_specs=[pl.BlockSpec(memory_space=out_space) for _ in outs],
        scratch_shapes=list(scratch),
        compiler_params=pltpu.CompilerParams(vmem_limit_bytes=limit * MIB),
        cost_estimate=pl.CostEstimate(flops=flops, bytes_accessed=size, transcendentals=0),
    )(*args)


def shape(dims, dtype=F32):
    return jax.ShapeDtypeStruct(tuple(dims), dtype)


def prepare(mean_operator, field_operators, adjacency, mode_masks, modes_dev, bits):
    layers, faces, blk, wide = mean_operator.shape
    ops = bits + 1
    full = faces * blk

    def layer_of(spot):
        lead = place()[1]
        return jnp.where(spot == 0, lead, 1 - lead)

    dense_spec = pl.BlockSpec((1, 1, full, full), lambda l, op, *_: (l, op, 0, 0))
    side_spec = pl.BlockSpec((1, 1, faces, blk, blk), lambda l, op, *_: (l, op, 0, 0, 0))
    grid_spec = pltpu.PrefetchScalarGridSpec(
        num_scalar_prefetch=2,
        grid=(layers, ops),
        in_specs=[
            pl.BlockSpec(
                (1, faces, blk, wide), lambda l, op, masks, adj: (layer_of(l), 0, 0, 0)
            ),
            pl.BlockSpec(
                (1, 1, faces, blk, wide),
                lambda l, op, masks, adj: (field_of(masks, op, modes_dev), layer_of(l), 0, 0, 0),
            ),
        ],
        out_specs=[dense_spec] * 2 + [side_spec] * 4,
        scratch_shapes=[pltpu.VMEM((faces, full, blk), F32)],
    )
    dense = shape((layers, ops, full, full), BF16)
    side = shape((layers, ops, faces, blk, blk), BF16)
    return pl.pallas_call(
        prepare_kernel,
        grid_spec=grid_spec,
        out_shape=[dense] * 2 + [side] * 4,
        compiler_params=pltpu.CompilerParams(vmem_limit_bytes=56 * MIB),
        cost_estimate=pl.CostEstimate(flops=10**8, bytes_accessed=36 * MIB, transcendentals=0),
    )(mode_masks, adjacency, mean_operator, field_operators)


def pair_list(count, modes, inner):
    half = modes // 2
    pairs = []
    for s in range(count):
        t = (s + 1 if (s % 2 == 0) == inner else s - 1) % count
        turn = half if ((s + 1) // 2 - (t + 1) // 2) % 2 else 0
        pairs += [(s * modes + m, t * modes + (m ^ turn)) for m in range(modes)]
    return pairs


def per_device(source_field, mean_operator, field_operators, adjacency, mode_masks):
    layers, faces, blk, modes_dev = source_field.shape
    count, modes = lax.axis_size("space"), lax.axis_size("mode")
    bits = modes.bit_length() - 1
    group = modes_dev // modes
    rows = modes * group
    pieces = shape((modes, layers, faces, group, blk))
    layer = shape((faces, rows, blk))

    (sent,) = call(
        split_kernel,
        [pieces],
        [source_field],
        limit=60,
        in_space=pltpu.HBM,
        out_space=pltpu.HBM,
        scratch=[
            pltpu.VMEM(source_field.shape, F32),
            pltpu.VMEM(pieces.shape, F32),
            pltpu.SemaphoreType.DMA((layers, faces)),
            pltpu.SemaphoreType.DMA((layers,)),
        ],
    )
    got = lax.all_to_all(sent, "mode", 0, 0, tiled=True)
    weights = prepare(
        mean_operator, field_operators, adjacency, mode_masks, modes_dev, bits
    )
    got, *weights = lax.optimization_barrier((got, *weights))
    dh, dl, hh, hl, ch, cl = weights
    b = [got[:, l].transpose(1, 0, 2, 3).reshape(faces, rows, blk) for l in range(layers)]

    links = [pair_list(count, modes, True), pair_list(count, modes, False)]
    sigma = THETA / DELTA
    rho = 1.0 / sigma
    d, r = [v / THETA for v in b], b
    flops = 2 * rows * blk * blk * 3 * (bits + 1) * faces
    for step in range(DEGREE):
        last = step == DEGREE - 1
        halo = [lax.ppermute(d[l], AXES, links[l]) for l in range(layers)]
        pre0, pre1, *x_next = call(
            functools.partial(local_kernel, group, step > 0),
            [layer] * (4 if step else 2),
            [*d, *r, *(x if step else []), dh, dl, ch, cl],
        )
        pre = [pre0, pre1]
        x = x_next if step else d
        rho_new = 1.0 / (2.0 * sigma - rho)
        coef = (rho_new * rho, 2.0 * rho_new / DELTA)
        rho = rho_new
        if not last:
            fresh = []
            for l in reversed(range(layers)):
                if fresh:
                    pre[l], _ = lax.optimization_barrier((pre[l], fresh[0][1]))
                fresh.append(
                    call(
                        functools.partial(finish_kernel, group, coef, l),
                        [layer, layer],
                        [halo[l], pre[l], hh, hl, d[l]],
                    )
                )
            fresh = fresh[::-1]
            r, d = zip(*fresh)
    (r_end,) = call(
        functools.partial(finish_kernel, group, None, 0), [layer], [halo[0], pre[0], hh, hl]
    )
    both = (modes, 2) + pieces.shape[1:]
    (send,) = call(
        functools.partial(last_kernel, group),
        [shape(both)],
        [halo[1], pre[1], r_end, *x, hh, hl],
        limit=12,
        out_space=pltpu.HBM,
        scratch=[pltpu.VMEM(both, F32), pltpu.SemaphoreType.DMA((2, layers))],
    )
    back = lax.all_to_all(send, "mode", 0, 0, tiled=True)
    field = shape(source_field.shape)
    return tuple(
        call(
            join_kernel,
            [field, field],
            [back],
            limit=12,
            out_space=pltpu.HBM,
            scratch=[
                pltpu.VMEM((2,) + source_field.shape, F32),
                pltpu.SemaphoreType.DMA((2, layers)),
            ],
        )
    )


def solution(mesh):
    in_specs = (
        P("space", None, None, "mode"),
        P("space", None, None, None),
        P(None, "space", None, None, None),
        P("space", None, None),
        P(),
    )
    out_specs = (P("space", None, None, "mode"), P("space", None, None, "mode"))
    return jax.shard_map(
        per_device, mesh=mesh, in_specs=in_specs, out_specs=out_specs, check_vma=False
    )
```
